256 devices in a mesh: row: 8 (over y, core), col: 32 (over z, x).
Axes of the slice: x: 4, y: 4, z: 8, core: 2. Of those that a mesh axis runs over, the one named last changes fastest.
Arguments:
- right_sides: bfloat16 [1024, 64, 256], P('col', 'row'), may hold values from -6 to 6
- prior_left: bfloat16 [64, 128, 48, 1024], P('row', 'col'), may hold values from -0.15625 to 0.15625
- prior_right: bfloat16 [64, 128, 48, 1024], P('row', 'col'), may hold values from -0.1875 to 0.1875
- solved_prior: bfloat16 [128, 1024, 256], P('col', 'row'), may hold values from -6 to 6
- diag_left: bfloat16 [64, 4, 48, 1024], P('row', None, None, 'col'), may hold values from -0.4375 to 0.4375
- diag_right: bfloat16 [64, 4, 48, 1024], P('row', None, None, 'col'), may hold values from -0.1875 to 0.1875
- diag_inverse: bfloat16 [4, 1024, 1024], P(None, 'col'), may hold values from -1 to 2, as said below
Outputs:
- updated: float32 [1024, 64, 256], P('col', 'row')
- solved: bfloat16 [4, 1024, 256], P(None, 'col')
The draws below stay inside these ranges and needn't reach their ends.
Inputs may be any that keep to these rules, and one draw needn't show every extreme that they name: `diag_inverse`: each tile is lower triangular.
All inputs are finite; a program needn't handle non-finite values.
Results may differ from the reference program's by a relative error of at most 0.012.
Values may be sent and summed in bfloat16 or wider, within the bound.
A program may use at most 64 MiB of HBM per device.

```python
import math
import jax
import jax.numpy as jnp
from jax import lax

TILE = 1024
RANK = 48
RHS = 256
STEPS = 4
RDEV = 8
ROWS = 64
PRIOR = 128
N_ROW = 8


def draw_diag_inverse(key, part):
    noise_key = jax.random.fold_in(key, 11)
    scale_key = jax.random.fold_in(key, 12)
    noise = jax.random.truncated_normal(noise_key, -4.0, 4.0, (STEPS, TILE, TILE), jnp.float32) * (0.5 / math.sqrt(TILE))
    lower = jnp.tril(noise, -1)
    scales = jax.random.uniform(scale_key, (STEPS, TILE), jnp.float32, 0.6, 1.6)
    eye_mat = jnp.eye(TILE, dtype=jnp.float32)
    return (lower + eye_mat[None, :, :] * scales[:, :, None]).astype(jnp.bfloat16)


def spiked(values, own_key, source, target, blocks, factor):
    def block_of(dim):
        return (jnp.arange(values.shape[dim]) // (values.shape[dim] // blocks)).reshape((-1,) + (1,) * (values.ndim - 1 - dim))

    one_side = jax.random.permutation(own_key, blocks)[block_of(target)]
    second = (block_of(target) + blocks // 2) % blocks
    return jnp.where((block_of(source) == one_side) | (block_of(source) == second), factor * values, values)


def steps_of(key, shape, cuts, smallest, high):
    loudness = 1.0
    for axis_at, parts in cuts:
        steps = jax.random.uniform(jax.random.fold_in(jax.random.fold_in(key, 6), axis_at), (parts,), jnp.float32, smallest / len(cuts), high / len(cuts))
        loudness = loudness * jnp.repeat(jnp.exp(steps), shape[axis_at] // parts).reshape((-1,) + (1,) * (len(shape) - 1 - axis_at))
    return loudness


def bell_draw(key, dims, spread, limit, pieces=(), kind=jnp.bfloat16):
    loudness = steps_of(key, dims, pieces, -0.22, 0.18) if pieces else 1.0
    entries = jax.random.normal(key, dims, jnp.float32) * spread * loudness
    return jnp.minimum(jnp.maximum(entries, -limit), limit).astype(kind)


def gaussian_with(stream_key, extent, width, reach, pieces, heavy, kind=jnp.bfloat16):
    drawn = width * jax.random.normal(stream_key, extent, jnp.float32)
    if pieces:
        drawn = drawn * steps_of(stream_key, extent, pieces, -0.22, 0.18)
    return jnp.clip(spiked(drawn, jax.random.fold_in(stream_key, 3), *heavy), -reach, reach).astype(kind)


def setup_inputs(seed: int = 0) -> dict:
    seeds = jax.random.split(jax.random.key(seed), 8)
    right_sides = bell_draw(seeds[0], (TILE, ROWS, RHS), 1.0, 6.0, ((0, 32), (1, 8)))
    prior_left = gaussian_with(seeds[1], (ROWS, PRIOR, RANK, TILE), (RANK * PRIOR) ** -0.5, 0.15625, ((0, 8), (1, 32)), (1, 3, 32, 2.75))
    prior_right = bell_draw(seeds[2], (ROWS, PRIOR, RANK, TILE), TILE ** -0.5, 0.1875, ((0, 8), (1, 32)))
    solved_prior = bell_draw(seeds[3], (PRIOR, TILE, RHS), 1.0, 6.0, ((0, 32), (1, 8)))
    diag_left = bell_draw(seeds[4], (ROWS, STEPS, RANK, TILE), (RANK * STEPS) ** -0.5, 0.4375, ((0, 8), (3, 32)))
    diag_right = bell_draw(seeds[5], (ROWS, STEPS, RANK, TILE), TILE ** -0.5, 0.1875, ((0, 8), (3, 32)))
    diag_inverse = draw_diag_inverse(jax.random.fold_in(seeds[7], 71), 0)
    return dict(right_sides=right_sides, prior_left=prior_left, prior_right=prior_right, solved_prior=solved_prior, diag_left=diag_left, diag_right=diag_right, diag_inverse=diag_inverse)


def tile_index(position):
    return (position % RDEV) * N_ROW + position // RDEV


def rounded(values):
    return lax.optimization_barrier(values.astype(jnp.bfloat16)).astype(jnp.float32)


def reference(right_sides, prior_left, prior_right, solved_prior, diag_left, diag_right, diag_inverse):
    known = solved_prior.astype(jnp.float32)

    def prior_row(factors):
        left_row, right_row = factors
        coeff = rounded(jnp.einsum("prt,pth->prh", right_row.astype(jnp.float32), known, precision=lax.Precision.HIGHEST))
        return jnp.einsum("prt,prh->th", left_row.astype(jnp.float32), coeff, precision=lax.Precision.HIGHEST)

    prior = lax.map(prior_row, (prior_left, prior_right))
    base = right_sides.astype(jnp.float32) - jnp.transpose(prior, (1, 0, 2))
    positions = jnp.arange(ROWS, dtype=jnp.int32)
    tiles = tile_index(positions)
    near_list = []
    solved_list = []
    for step in range(STEPS):
        spot = step * RDEV
        current = base[:, spot]
        for earlier in range(step):
            current = current - jnp.einsum("rt,rh->th", diag_left[spot, earlier].astype(jnp.float32), near_list[earlier][spot], precision=lax.Precision.HIGHEST)
        answer = jnp.dot(diag_inverse[step], current.astype(jnp.bfloat16), preferred_element_type=jnp.float32).astype(jnp.bfloat16)
        solved_list.append(answer)
        near_list.append(rounded(jnp.einsum("irt,th->irh", diag_right[:, step].astype(jnp.float32), answer.astype(jnp.float32), precision=lax.Precision.HIGHEST)))
    total = jnp.zeros(base.shape, jnp.float32)
    for step in range(STEPS):
        gate = (tiles > step).astype(jnp.float32)
        total = total + jnp.einsum("irt,irh->tih", diag_left[:, step].astype(jnp.float32), near_list[step] * gate[:, None, None], precision=lax.Precision.HIGHEST)
    return base - total, jnp.stack(solved_list, 0)
```

```python
import jax
import jax.numpy as jnp
from jax import lax
from jax.experimental import pallas as pl
from jax.experimental.pallas import tpu as pltpu
from jax.sharding import PartitionSpec as P

ROW = "row"
COL = "col"
CORES = 2
NX = 4
MESH = pl.DeviceIdType.MESH
F32 = jnp.float32
BF16 = jnp.bfloat16
GROUPS = ((0,), (1, 2, 3), (4, 5, 6, 7))


def remote(src, dst, send, recv, row, col):
    return pltpu.make_async_remote_copy(
        src_ref=src,
        dst_ref=dst,
        send_sem=send,
        recv_sem=recv,
        device_id={ROW: row, COL: col},
        device_id_type=MESH,
    )


def prior_kernel(left_in, right_in, known_in, out, left, right, known, coeff, *rest):
    rows, cols = lax.axis_size(ROW), lax.axis_size(COL)
    ny, nz = rows // CORES, cols // NX
    count = len(GROUPS)
    parts, from_a, from_b, from_l, from_r, part_sum, from_z = (
        rest[i * count : (i + 1) * count] for i in range(7)
    )
    local_sem, gather_send, gather_recv, x_send, x_recv, z_send, z_recv = rest[7 * count :]
    r, c = lax.axis_index(ROW), lax.axis_index(COL)
    y, q = r // CORES, r % CORES
    z, x = c // NX, c % NX
    up, down, far = (((y + d) % ny) * CORES + q for d in (1, ny - 1, 2))
    partner = y * CORES + 1 - q
    right_x, left_x, far_x = ((x + d) % NX for d in (1, NX - 1, 2))
    depth = known_in.shape[1]
    priors = known_in.shape[0]
    rank = left_in.shape[2]

    loads = [
        pltpu.make_async_copy(known_in, known.at[:, pl.ds(r * depth, depth)], local_sem.at[0]),
        pltpu.make_async_copy(right_in, right, local_sem.at[1]),
        pltpu.make_async_copy(left_in, left, local_sem.at[2]),
    ]
    for load in loads:
        load.start()
    barrier = pltpu.get_barrier_semaphore()
    peers = [(up, c), (down, c), (partner, c), (r, z * NX + right_x), (r, z * NX + left_x)]
    peers += [(r, ((z + d) % nz) * NX + x) for d in range(1, nz)]
    for row, col in peers:
        pl.semaphore_signal(barrier, inc=1, device_id={ROW: row, COL: col}, device_id_type=MESH)
    pl.semaphore_wait(barrier, len(peers))
    loads[0].wait()

    sends = []

    def go(copy):
        copy.start()
        sends.append(copy)
        return copy

    def block(row, j):
        return known.at[j, pl.ds(row * depth, depth)]

    def share(row_of_block, j, kind, target):
        return remote(
            block(row_of_block, j), block(row_of_block, j), gather_send.at[kind, j], gather_recv.at[kind, j], target, c
        )

    own_up, own_down, relay, over = [], [], [], [[], [], [], []]
    for j in range(priors):
        own_up.append(go(share(r, j, 0, up)))
        own_down.append(go(share(r, j, 1, down)))
        over[0].append(go(share(r, j, 3, partner)))
    for j in range(priors):
        own_up[j].wait_recv()
        over[1].append(go(share(down, j, 4, partner)))
        if j < priors // 2:
            relay.append(go(share(down, j, 2, up)))
        own_down[j].wait_recv()
        over[2].append(go(share(up, j, 5, partner)))
        if j >= priors // 2:
            relay.append(go(share(up, j, 2, down)))
    for load in loads[1:]:
        load.wait()
    for j in range(priors):
        relay[j].wait_recv()
        over[3].append(go(share(far, j, 6, partner)))
        for kind in range(4):
            over[kind][j].wait_recv()
        factors = right[:, j].reshape(-1, right.shape[3])
        product = jnp.dot(factors, known[j], preferred_element_type=F32)
        coeff[:, pl.ds(j * rank, rank)] = product.astype(BF16).reshape(-1, rank, product.shape[1])

    def multiply(g):
        first = GROUPS[g][0]

        def one(at, carry):
            a = at + first
            factors = left[a].reshape(priors * rank, -1)
            term = lax.dot_general(factors, coeff[a], (((0,), (0,)), ((), ())), preferred_element_type=F32)
            term = term.astype(BF16).reshape(nz, NX, -1, term.shape[1])
            for at_x in range(NX):
                parts[g][at_x, :, at] = term[:, at_x]
            return carry

        lax.fori_loop(0, len(GROUPS[g]), one, 0)

    low, high = pl.ds(0, nz // 2), pl.ds(nz // 2, nz // 2)
    steps = [dict() for _ in GROUPS]

    def send_x(g, kind, src, dst, target_x):
        return go(remote(src, dst, x_send.at[g, kind], x_recv.at[g, kind], r, z * NX + target_x))

    def x_first(g):
        steps[g]["a"] = send_x(g, 0, parts[g].at[far_x, low], from_a[g], right_x)
        steps[g]["b"] = send_x(g, 1, parts[g].at[far_x, high], from_b[g], left_x)
        steps[g]["l0"] = send_x(g, 2, parts[g].at[right_x, high], from_l[g].at[high], right_x)
        steps[g]["r0"] = send_x(g, 3, parts[g].at[left_x, low], from_r[g].at[low], left_x)

    def x_second(g):
        steps[g]["a"].wait_recv()
        parts[g][right_x, low] = (parts[g][right_x, low].astype(F32) + from_a[g][...].astype(F32)).astype(BF16)
        steps[g]["l1"] = send_x(g, 4, parts[g].at[right_x, low], from_l[g].at[low], right_x)
        steps[g]["b"].wait_recv()
        parts[g][left_x, high] = (parts[g][left_x, high].astype(F32) + from_b[g][...].astype(F32)).astype(BF16)
        steps[g]["r1"] = send_x(g, 5, parts[g].at[left_x, high], from_r[g].at[high], left_x)

    def z_all(g):
        for name in ("l0", "r0", "l1", "r1"):
            steps[g][name].wait_recv()

        def one(at, carry):
            total = parts[g][x, at].astype(F32) + from_l[g][at].astype(F32) + from_r[g][at].astype(F32)
            part_sum[g][at] = total.astype(BF16)
            return carry

        lax.fori_loop(0, nz, one, 0)
        steps[g]["z"] = []
        for d in range(1, nz):
            to = (z + d) % nz
            steps[g]["z"].append(
                go(remote(part_sum[g].at[to], from_z[g].at[d], z_send.at[g, d], z_recv.at[g, d], r, to * NX + x))
            )

    def finish(g):
        total = part_sum[g][z].astype(F32)
        for d in range(1, nz):
            steps[g]["z"][d - 1].wait_recv()
        for d in range(1, nz):
            total = total + from_z[g][d].astype(F32)
        out[pl.ds(GROUPS[g][0], len(GROUPS[g]))] = total

    multiply(0)
    x_first(0)
    multiply(1)
    x_first(1)
    x_second(0)
    multiply(2)
    x_first(2)
    z_all(0)
    x_second(1)
    finish(0)
    z_all(1)
    x_second(2)
    finish(1)
    z_all(2)
    finish(2)
    for copy in sends:
        copy.wait_send()


def prior_sums(prior_left, prior_right, solved_prior):
    local_rows, priors, rank, tile = prior_left.shape
    sides = solved_prior.shape[2]
    cols = lax.axis_size(COL)
    nz = cols // NX
    depth = tile // cols

    def buffers(*lead):
        return [pltpu.VMEM((*lead, len(group), depth, sides), BF16) for group in GROUPS]

    count = len(GROUPS)
    scratch = [
        pltpu.VMEM(prior_left.shape, BF16),
        pltpu.VMEM(prior_right.shape, BF16),
        pltpu.VMEM((priors, tile, sides), BF16),
        pltpu.VMEM((local_rows, priors * rank, sides), BF16),
        *buffers(NX, nz),
        *buffers(nz // 2),
        *buffers(nz // 2),
        *buffers(nz),
        *buffers(nz),
        *buffers(nz),
        *buffers(nz),
        pltpu.SemaphoreType.DMA((3,)),
        pltpu.SemaphoreType.DMA((7, priors)),
        pltpu.SemaphoreType.DMA((7, priors)),
        pltpu.SemaphoreType.DMA((count, 6)),
        pltpu.SemaphoreType.DMA((count, 6)),
        pltpu.SemaphoreType.DMA((count, nz)),
        pltpu.SemaphoreType.DMA((count, nz)),
    ]
    return pl.pallas_call(
        prior_kernel,
        out_shape=jax.ShapeDtypeStruct((local_rows, depth, sides), F32),
        in_specs=[pl.BlockSpec(memory_space=pl.ANY)] * 3,
        out_specs=pl.BlockSpec(memory_space=pltpu.VMEM),
        scratch_shapes=scratch,
        compiler_params=pltpu.CompilerParams(
            collective_id=0, has_side_effects=True, vmem_limit_bytes=48 * 1024 * 1024
        ),
    )(prior_left, prior_right, solved_prior)


def copy_for_each(value, axis):
    count = lax.axis_size(axis)
    return lax.all_to_all(
        jnp.broadcast_to(value[None], (count, *value.shape)), axis, 0, 0, tiled=True
    )


def laid_out(blocks, dim):
    lengths = list(blocks.shape[1:])
    lengths[dim] *= blocks.shape[0]
    return jnp.moveaxis(blocks, 0, dim).reshape(lengths)


def collect(value, axis, dim):
    return laid_out(copy_for_each(value, axis), dim)


def picked(value, axis, root):
    return lax.dynamic_index_in_dim(lax.all_gather(value, axis), root, 0, keepdims=False)


def cut_along(value, dim, count):
    before, after = (value.shape[:dim], value.shape[dim + 1 :])
    return jnp.moveaxis(value.reshape(*before, count, -1, *after), dim, 0)


def summed_on_arrival(value, axis, dim):
    count = lax.axis_size(axis)
    blocks = lax.all_to_all(cut_along(value, dim, count), axis, 0, 0, tiled=True)
    return jnp.sum(blocks, axis=0)


def padded_to(lines, count):
    spare = -len(lines) % count
    return jnp.pad(lines, [(0, spare)] + [(0, 0)] * (lines.ndim - 1))


def sum_by_parts(value, axes):
    lines = value.reshape(-1, value.shape[-1])
    own = summed_on_arrival(padded_to(lines, lax.axis_size(axes)), axes, 0)
    whole = collect(own, axes, 0)
    return whole[: len(lines)].reshape(value.shape)


def local(right_sides, prior_left, prior_right, solved_prior, diag_left, diag_right, diag_inverse):
    slice_rows = right_sides.shape[0]
    local_rows = right_sides.shape[1]
    sides_count = right_sides.shape[2]
    steps_count = diag_left.shape[1]
    row_index = lax.axis_index(ROW)
    prior = prior_sums(prior_left, prior_right, solved_prior)
    base = right_sides.astype(F32) - jnp.swapaxes(prior, 0, 1)
    leading = base[:, 0]
    solved_list = []
    trailing = jnp.zeros((slice_rows, local_rows - 1, sides_count), F32)
    for step in range(steps_count):
        block = diag_inverse[step]
        answer = jnp.dot(
            block, collect(leading.astype(BF16), COL, 0), preferred_element_type=F32
        ).astype(BF16)
        answer = picked(answer, ROW, step)
        solved_list.append(answer)
        all_terms = jnp.einsum("art,th->arh", diag_right[:, step], answer, preferred_element_type=F32)
        all_coeff = sum_by_parts(all_terms, COL).astype(BF16)
        first_coeff = all_coeff[0]
        trailing = trailing + jnp.einsum(
            "art,arh->tah", diag_left[1:, step], all_coeff[1:], preferred_element_type=F32
        )
        gate = (row_index > step).astype(F32)
        leading = leading - gate * jnp.einsum(
            "rt,rh->th", diag_left[0, step], first_coeff, preferred_element_type=F32
        )
    others = base[:, 1:] - trailing
    updated = jnp.concatenate([leading[:, None, :], others], axis=1)
    return (updated, jnp.stack(solved_list, 0))


def solution(mesh):
    return jax.shard_map(
        local,
        mesh=mesh,
        in_specs=(
            P(COL, ROW, None),
            P(ROW, COL, None, None),
            P(ROW, COL, None, None),
            P(COL, ROW, None),
            P(ROW, None, None, COL),
            P(ROW, None, None, COL),
            P(None, COL, None),
        ),
        out_specs=(P(COL, ROW, None), P(None, COL, None)),
        check_vma=False,
    )
```

```python
import jax
import jax.numpy as jnp
from jax import lax
from jax.experimental import pallas as pl
from jax.experimental.pallas import tpu as pltpu
from jax.sharding import PartitionSpec as P

ROW = "row"
COL = "col"
CORES = 2
NX = 4
MESH = pl.DeviceIdType.MESH
F32 = jnp.float32
BF16 = jnp.bfloat16
LANES = 128
GROUPS = ((0,), (1, 2, 3), (4, 5, 6, 7))
LEAD_PAIRS = ((1, 0), (2, 0), (3, 0), (2, 1), (3, 1), (3, 2))
CROSS_PAIRS = ((2, 1), (3, 1), (3, 2))
CHUNK = 16
TN = (((0,), (0,)), ((), ()))
NT = (((1,), (1,)), ((), ()))


def dot(a, b, dims=None):
    if dims is None:
        return jnp.dot(a, b, preferred_element_type=F32)
    return lax.dot_general(a, b, dims, preferred_element_type=F32)


def remote(src, dst, send, recv, row, col):
    return pltpu.make_async_remote_copy(
        src_ref=src,
        dst_ref=dst,
        send_sem=send,
        recv_sem=recv,
        device_id={ROW: row, COL: col},
        device_id_type=MESH,
    )


class Place:
    def __init__(self):
        self.rows, self.cols = lax.axis_size(ROW), lax.axis_size(COL)
        self.ny, self.nz = self.rows // CORES, self.cols // NX
        self.r, self.c = lax.axis_index(ROW), lax.axis_index(COL)
        self.y, self.q = self.r // CORES, self.r % CORES
        self.z, self.x = self.c // NX, self.c % NX
        self.up, self.down, self.far = (((self.y + d) % self.ny) * CORES + self.q for d in (1, self.ny - 1, 2))
        self.partner = self.y * CORES + 1 - self.q
        self.right_x, self.left_x, self.far_x = ((self.x + d) % NX for d in (1, NX - 1, 2))
        self.low, self.high = pl.ds(0, self.nz // 2), pl.ds(self.nz // 2, self.nz // 2)
        self.sends = []

    def go(self, copy):
        copy.start()
        self.sends.append(copy)
        return copy

    def along_x(self, target):
        return self.z * NX + target

    def along_z(self, d):
        return ((self.z + d) % self.nz) * NX + self.x


class Reduce:
    def __init__(self, at, buffers, sems):
        self.at = at
        self.parts, self.from_a, self.from_b, self.from_l, self.from_r, self.part_sum, self.from_z = buffers
        self.x_send, self.x_recv, self.z_send, self.z_recv = sems
        self.copies = {}
        self.z_copies = []

    def send_x(self, kind, src, dst, target_x):
        at = self.at
        copy = remote(src, dst, self.x_send.at[kind], self.x_recv.at[kind], at.r, at.along_x(target_x))
        self.copies[kind] = at.go(copy)

    def first(self):
        at = self.at
        self.send_x(0, self.parts.at[at.far_x, at.low], self.from_a, at.right_x)
        self.send_x(1, self.parts.at[at.far_x, at.high], self.from_b, at.left_x)
        self.send_x(2, self.parts.at[at.right_x, at.high], self.from_l.at[at.high], at.right_x)
        self.send_x(3, self.parts.at[at.left_x, at.low], self.from_r.at[at.low], at.left_x)

    def second(self):
        at = self.at
        self.copies[0].wait_recv()
        own = self.parts[at.right_x, at.low].astype(F32)
        self.parts[at.right_x, at.low] = (own + self.from_a[...].astype(F32)).astype(BF16)
        self.send_x(4, self.parts.at[at.right_x, at.low], self.from_l.at[at.low], at.right_x)
        self.copies[1].wait_recv()
        own = self.parts[at.left_x, at.high].astype(F32)
        self.parts[at.left_x, at.high] = (own + self.from_b[...].astype(F32)).astype(BF16)
        self.send_x(5, self.parts.at[at.left_x, at.high], self.from_r.at[at.high], at.left_x)

    def third(self):
        at = self.at
        for kind in range(2, 6):
            self.copies[kind].wait_recv()

        def one(i, carry):
            total = self.parts[at.x, i].astype(F32) + self.from_l[i].astype(F32) + self.from_r[i].astype(F32)
            self.part_sum[i] = total.astype(BF16)
            return carry

        lax.fori_loop(0, at.nz, one, 0)
        for d in range(1, at.nz):
            src = self.part_sum.at[(at.z + d) % at.nz]
            copy = remote(src, self.from_z.at[d], self.z_send.at[d], self.z_recv.at[d], at.r, at.along_z(d))
            self.z_copies.append(at.go(copy))

    def result(self):
        at = self.at
        for copy in self.z_copies:
            copy.wait_recv()
        total = self.part_sum[at.z].astype(F32)
        for d in range(1, at.nz):
            total = total + self.from_z[d].astype(F32)
        return total


class Gather:
    def __init__(self, at, whole, sems):
        self.at = at
        self.whole = whole
        self.z_send, self.z_recv, self.x_send, self.x_recv = sems

    def z_copy(self, d):
        at = self.at
        own = self.whole.at[at.z, at.x]
        return remote(own, own, self.z_send.at[d], self.z_recv.at[d], at.r, at.along_z(d))

    def x_copy(self, kind):
        at, whole = self.at, self.whole
        part, target = (
            (whole.at[:, at.x], at.right_x),
            (whole.at[:, at.x], at.left_x),
            (whole.at[at.low, at.left_x], at.right_x),
            (whole.at[at.high, at.right_x], at.left_x),
        )[kind]
        return remote(part, part, self.x_send.at[kind], self.x_recv.at[kind], at.r, at.along_x(target))

    def first(self):
        for d in range(1, self.at.nz):
            self.z_copy(d).start()

    def second(self):
        for d in range(1, self.at.nz):
            self.z_copy(d).wait_recv()
        for kind in (0, 1):
            self.x_copy(kind).start()

    def third(self):
        for kind in (0, 1):
            self.x_copy(kind).wait_recv()
            self.x_copy(kind + 2).start()

    def wait(self):
        for kind in (2, 3):
            self.x_copy(kind).wait_recv()

    def close(self):
        for d in range(1, self.at.nz):
            self.z_copy(d).wait_send()
        for kind in range(4):
            self.x_copy(kind).wait_send()


def take(refs, count):
    return [refs.pop(0) for _ in range(count)]


def kernel(sides_in, left_in, right_in, known_in, dleft_in, dright_in, inverse_in, updated, solved, *scratch):
    at = Place()
    r, c, go = at.r, at.c, at.go
    refs = list(scratch)
    left, right, known, coeff, sides, dleft, dright, inverse = take(refs, 8)
    packs, lead_left, base_whole, near_whole, cross_whole = take(refs, 5)
    start, wide, lead_coeff, near = take(refs, 4)
    reduce_buffers = [take(refs, 7) for _ in range(len(GROUPS) + 2)]
    load_sem, gather_send, gather_recv, x_send, x_recv, z_send, z_recv = take(refs, 7)
    all_z_send, all_z_recv, all_x_send, all_x_recv = take(refs, 4)
    pack_send, pack_recv, start_send, start_recv = take(refs, 4)

    depth, priors = known_in.shape[1], known_in.shape[0]
    local_rows, steps, rank, thin = dleft.shape
    sides_count = sides.shape[2]
    tile = left.shape[3]
    width = steps * rank
    half = packs.shape[2] // 2

    def sems(i):
        return x_send.at[i], x_recv.at[i], z_send.at[i], z_recv.at[i]

    def all_sems(i):
        return all_z_send.at[i], all_z_recv.at[i], all_x_send.at[i], all_x_recv.at[i]

    prior = [Reduce(at, reduce_buffers[i], sems(i)) for i in range(len(GROUPS))]
    near_sum = Reduce(at, reduce_buffers[-2], sems(len(GROUPS)))
    cross_sum = Reduce(at, reduce_buffers[-1], sems(len(GROUPS) + 1))
    lead_all = Gather(at, lead_left, all_sems(0))
    base_all = Gather(at, base_whole, all_sems(1))
    near_all = Gather(at, near_whole, all_sems(2))
    cross_all = Gather(at, cross_whole, all_sems(3))

    loads = [
        pltpu.make_async_copy(src, dst, load_sem.at[i])
        for i, (src, dst) in enumerate(
            (
                (known_in, known.at[:, pl.ds(r * depth, depth)]),
                (dleft_in, dleft),
                (dright_in, dright),
                (right_in, right),
                (left_in, left),
                (inverse_in, inverse),
                (sides_in, sides),
            )
        )
    ]
    for load in loads:
        load.start()
    barrier = pltpu.get_barrier_semaphore()
    peers = [((r + d) % at.rows, c) for d in range(1, at.rows)]
    peers += [(r, at.along_x(at.right_x)), (r, at.along_x(at.left_x))]
    peers += [(r, at.along_z(d)) for d in range(1, at.nz)]
    for row, col in peers:
        pl.semaphore_signal(barrier, inc=1, device_id={ROW: row, COL: col}, device_id_type=MESH)

    for load in loads[1:3]:
        load.wait()
    eye = (
        lax.broadcasted_iota(jnp.int32, (thin, thin), 0) == lax.broadcasted_iota(jnp.int32, (thin, thin), 1)
    ).astype(BF16)
    packs[r] = jnp.zeros(packs.shape[1:], BF16)
    packs[r, :, :width] = dot(eye, dleft[0].reshape(width, thin), NT).astype(BF16)
    packs[r, :, half : half + width] = dot(eye, dright[0].reshape(width, thin), NT).astype(BF16)
    loads[0].wait()
    pl.semaphore_wait(barrier, len(peers))

    def block(row, j):
        return known.at[j, pl.ds(row * depth, depth)]

    def share(row_of_block, j, kind, target):
        part = block(row_of_block, j)
        return remote(part, part, gather_send.at[kind, j], gather_recv.at[kind, j], target, c)

    own_up, own_down, relay, over = [], [], [], [[], [], [], []]
    for j in range(priors):
        own_up.append(go(share(r, j, 0, at.up)))
        own_down.append(go(share(r, j, 1, at.down)))
        over[0].append(go(share(r, j, 3, at.partner)))
    pack_copies = [
        go(remote(packs.at[r], packs.at[r], pack_send.at[d], pack_recv.at[d], (r + d) % at.rows, c))
        for d in range(1, at.rows)
    ]
    for j in range(priors):
        own_up[j].wait_recv()
        over[1].append(go(share(at.down, j, 4, at.partner)))
        if j < priors // 2:
            relay.append(go(share(at.down, j, 2, at.up)))
        own_down[j].wait_recv()
        over[2].append(go(share(at.up, j, 5, at.partner)))
        if j >= priors // 2:
            relay.append(go(share(at.up, j, 2, at.down)))

    for copy in pack_copies:
        copy.wait_recv()
    firsts = (None, 0, LANES, 2 * LANES)
    lead_left[at.z, at.x] = jnp.zeros(lead_left.shape[2:], BF16)
    for k in range(1, steps):
        lead_left[at.z, at.x, :, firsts[k] : firsts[k] + k * rank] = packs[k, :, : k * rank]
    lead_all.first()

    for load in loads[3:]:
        load.wait()
    for j in range(priors):
        relay[j].wait_recv()
        over[3].append(go(share(at.far, j, 6, at.partner)))
        for kind in range(4):
            over[kind][j].wait_recv()
        product = dot(right[:, j].reshape(-1, tile), known[j])
        coeff[:, pl.ds(j * rank, rank)] = product.astype(BF16).reshape(local_rows, rank, sides_count)

    def multiply(g):
        first = GROUPS[g][0]

        def one(i, carry):
            term = dot(left[i + first].reshape(priors * rank, tile), coeff[i + first], TN)
            term = term.astype(BF16).reshape(at.nz, NX, thin, sides_count)
            for at_x in range(NX):
                prior[g].parts[at_x, :, i] = term[:, at_x]
            return carry

        lax.fori_loop(0, len(GROUPS[g]), one, 0)

    def own_base(g):
        total = prior[g].result()
        for i, a in enumerate(GROUPS[g]):
            updated[a] = sides[a].astype(F32) - total[i]

    multiply(0)
    prior[0].first()
    lead_all.second()
    multiply(1)
    prior[0].second()
    lead_all.third()
    prior[1].first()
    prior[0].third()
    lead_all.wait()

    def lanes_of(m):
        return slice(firsts[m], firsts[m] + (LANES if m < 3 else 2 * LANES))

    whole_left = lead_left[...].reshape(tile, lead_left.shape[3])
    for m in range(1, steps):
        wide[:, lanes_of(m)] = dot(inverse[m], whole_left[:, lanes_of(m)]).astype(BF16)
    own_base(0)

    @pl.when(r < steps)
    def _():
        base_whole[at.z, at.x] = updated[0].astype(BF16)
        base_all.first()

    for m in range(1, steps):
        product = dot(dright[:, m].reshape(local_rows * rank, thin), wide[:, lanes_of(m)])
        product = product.astype(BF16).reshape(local_rows, rank, -1)
        cross_sum.parts[m, :, :rank] = product[:, :, :LANES]
        if m == 3:
            cross_sum.parts[0, :, :rank] = product[:, :, LANES:]

    def spread(target, pairs, right_of):
        chunks = []
        for k, m in pairs:
            factors = packs[k, :, half : half + width]
            product = dot(factors, right_of(m), TN)[m * rank : (m + 1) * rank]
            chunks += [product[i : i + CHUNK] for i in range(0, rank, CHUNK)]
        for i in range(at.cols):
            part = chunks[i].astype(BF16) if i < len(chunks) else jnp.zeros((CHUNK, target.parts.shape[3]), BF16)
            target.parts[i % NX, i // NX, rank:] = part

    spread(cross_sum, CROSS_PAIRS, lambda m: wide[:, lanes_of(m)])
    cross_sum.first()

    @pl.when(r < steps)
    def _():
        base_all.second()

    cross_sum.second()

    @pl.when(r < steps)
    def _():
        base_all.third()

    multiply(2)

    def start_copy(k, d):
        return remote(start.at[k], start.at[k], start_send.at[d], start_recv.at[k], (r + d) % at.rows, c)

    @pl.when(r < steps)
    def _():
        base_all.wait()
        start[r] = dot(inverse[r], base_whole[...].reshape(tile, sides_count)).astype(BF16)
        for d in range(1, at.rows):
            start_copy(r, d).start()

    cross_sum.third()
    prior[2].first()
    prior[1].second()
    for k in range(steps):

        @pl.when(r != k)
        def _():
            start_copy(k, 1).wait_recv()

    for m in range(steps):
        product = dot(dright[:, m].reshape(local_rows * rank, thin), start[m])
        near_sum.parts[m, :, :rank] = product.astype(BF16).reshape(local_rows, rank, sides_count)
    spread(near_sum, LEAD_PAIRS, lambda m: start[m])
    near_sum.first()
    cross_whole[at.z, at.x] = cross_sum.result().astype(BF16)
    cross_all.first()
    near_sum.second()
    prior[1].third()
    prior[2].second()
    cross_all.second()
    near_sum.third()
    cross_all.third()
    near_whole[at.z, at.x] = near_sum.result().astype(BF16)
    near_all.first()
    own_base(1)
    prior[2].third()
    near_all.second()
    near_all.third()
    own_base(2)
    cross_all.wait()
    near_all.wait()

    def lead_rows(whole, i):
        return jnp.concatenate(
            [whole[(3 * i + n) // NX, (3 * i + n) % NX, rank:].astype(F32) for n in range(3)], axis=0
        )

    for m in range(1, steps):
        lead_coeff[m] = jnp.zeros(lead_coeff.shape[1:], BF16)
    for i, (k, m) in enumerate(LEAD_PAIRS):
        value = lead_rows(near_whole, i)
        if m:
            cross = lead_rows(cross_whole, CROSS_PAIRS.index((k, m))).astype(BF16)
            value = value - dot(cross, lead_coeff[m, :LANES])
        lead_coeff[k, m * rank : (m + 1) * rank] = value.astype(BF16)

    for m in range(steps):
        answer = start[m].astype(F32)
        terms = near_whole[:, m, :rank].reshape(local_rows * rank, sides_count).astype(F32)
        if m:
            lanes = LANES if m < 3 else 2 * LANES
            answer = answer - dot(wide[:, lanes_of(m)], lead_coeff[m, :lanes])
            cross = cross_whole[:, m, :rank].reshape(local_rows * rank, LANES)
            terms = terms - dot(cross, lead_coeff[m, :LANES])
            if m == 3:
                cross = cross_whole[:, 0, :rank].reshape(local_rows * rank, LANES)
                terms = terms - dot(cross, lead_coeff[m, LANES:])
        solved[m] = answer.astype(BF16)
        near[:, m * rank : (m + 1) * rank] = terms.astype(BF16).reshape(local_rows, rank, sides_count)
    for m in range(steps):

        @pl.when(r <= m)
        def _():
            near[0, m * rank : (m + 1) * rank] = jnp.zeros((rank, sides_count), BF16)

    def last(a, carry):
        updated[a] = updated[a] - dot(dleft[a].reshape(width, thin), near[a], TN)
        return carry

    lax.fori_loop(0, local_rows, last, 0)

    for copy in at.sends:
        copy.wait_send()
    for gather in (lead_all, near_all, cross_all):
        gather.close()

    @pl.when(r < steps)
    def _():
        base_all.close()
        for d in range(1, at.rows):
            start_copy(r, d).wait_send()


def local(right_sides, prior_left, prior_right, solved_prior, diag_left, diag_right, diag_inverse):
    thin, local_rows, sides = right_sides.shape
    priors, rank, tile = prior_left.shape[1:]
    steps = diag_left.shape[1]
    rows, cols = lax.axis_size(ROW), lax.axis_size(COL)
    nz = cols // NX
    block = rank + CHUNK

    def reduce_scratch(*shape):
        return [
            pltpu.VMEM((*lead, *shape), BF16)
            for lead in ((NX, nz), (nz // 2,), (nz // 2,), (nz,), (nz,), (nz,), (nz,))
        ]

    count = len(GROUPS) + 2
    scratch = [
        pltpu.VMEM(prior_left.shape, BF16),
        pltpu.VMEM(prior_right.shape, BF16),
        pltpu.VMEM((priors, tile, sides), BF16),
        pltpu.VMEM((local_rows, priors * rank, sides), BF16),
        pltpu.VMEM((local_rows, thin, sides), BF16),
        pltpu.VMEM(diag_left.shape, BF16),
        pltpu.VMEM(diag_right.shape, BF16),
        pltpu.VMEM(diag_inverse.shape, BF16),
        pltpu.VMEM((rows, thin, 4 * LANES), BF16),
        pltpu.VMEM((nz, NX, thin, 4 * LANES), BF16),
        pltpu.VMEM((nz, NX, thin, sides), BF16),
        pltpu.VMEM((nz, NX, block, sides), BF16),
        pltpu.VMEM((nz, NX, block, LANES), BF16),
        pltpu.VMEM((steps, thin, sides), BF16),
        pltpu.VMEM((thin, 4 * LANES), BF16),
        pltpu.VMEM((steps, 2 * LANES, sides), BF16),
        pltpu.VMEM((local_rows, steps * rank, sides), BF16),
    ]
    for group in GROUPS:
        scratch += reduce_scratch(len(group), thin, sides)
    scratch += reduce_scratch(block, sides)
    scratch += reduce_scratch(block, LANES)
    for shape in (
        (7,),
        (7, priors),
        (7, priors),
        (count, 6),
        (count, 6),
        (count, nz),
        (count, nz),
        (4, nz),
        (4, nz),
        (4, 4),
        (4, 4),
        (rows,),
        (rows,),
        (rows,),
        (steps,),
    ):
        scratch.append(pltpu.SemaphoreType.DMA(shape))
    updated, solved = pl.pallas_call(
        kernel,
        out_shape=(
            jax.ShapeDtypeStruct((local_rows, thin, sides), F32),
            jax.ShapeDtypeStruct((steps, thin, sides), BF16),
        ),
        in_specs=[pl.BlockSpec(memory_space=pl.ANY)] * 7,
        out_specs=(pl.BlockSpec(memory_space=pltpu.VMEM), pl.BlockSpec(memory_space=pltpu.VMEM)),
        scratch_shapes=scratch,
        compiler_params=pltpu.CompilerParams(
            collective_id=0, has_side_effects=True, vmem_limit_bytes=56 * 1024 * 1024
        ),
    )(
        jnp.swapaxes(right_sides, 0, 1),
        prior_left,
        prior_right,
        solved_prior,
        diag_left,
        diag_right,
        diag_inverse,
    )
    return jnp.swapaxes(updated, 0, 1), solved


def solution(mesh):
    return jax.shard_map(
        local,
        mesh=mesh,
        in_specs=(
            P(COL, ROW, None),
            P(ROW, COL, None, None),
            P(ROW, COL, None, None),
            P(COL, ROW, None),
            P(ROW, None, None, COL),
            P(ROW, None, None, COL),
            P(None, COL, None),
        ),
        out_specs=(P(COL, ROW, None), P(None, COL, None)),
        check_vma=False,
    )
```

```python
import jax
import jax.numpy as jnp
from jax import lax
from jax.experimental import pallas as pl
from jax.experimental.pallas import tpu as pltpu
from jax.sharding import PartitionSpec as P

ROW = "row"
COL = "col"
CORES = 2
NX = 4
MESH = pl.DeviceIdType.MESH
F32 = jnp.float32
BF16 = jnp.bfloat16
LANES = 128
GROUPS = ((0,), (1, 2, 3), (4, 5, 6, 7))
CHUNK = 24
TN = (((0,), (0,)), ((), ()))


def dot(a, b, dims=None):
    if dims is None:
        return jnp.dot(a, b, preferred_element_type=F32)
    return lax.dot_general(a, b, dims, preferred_element_type=F32)


def remote(src, dst, send, recv, row, col):
    return pltpu.make_async_remote_copy(
        src_ref=src,
        dst_ref=dst,
        send_sem=send,
        recv_sem=recv,
        device_id={ROW: row, COL: col},
        device_id_type=MESH,
    )


class Copy:
    def __init__(self, copy, only=None):
        self.copy, self.only, self.landed = copy, only, False

    def wait_recv(self):
        self.copy.wait_recv()
        self.landed = True

    def close(self):
        def rest():
            if not self.landed:
                self.copy.wait_recv()
            self.copy.wait_send()

        if self.only is None:
            rest()
        else:
            pl.when(self.only)(rest)


class Place:
    def __init__(self):
        self.rows, self.cols = lax.axis_size(ROW), lax.axis_size(COL)
        self.ny, self.nz = self.rows // CORES, self.cols // NX
        self.r, self.c = lax.axis_index(ROW), lax.axis_index(COL)
        self.y, self.q = self.r // CORES, self.r % CORES
        self.z, self.x = self.c // NX, self.c % NX
        self.up, self.down, self.far = (((self.y + d) % self.ny) * CORES + self.q for d in (1, self.ny - 1, 2))
        self.partner = self.y * CORES + 1 - self.q
        self.next_x = [(self.x + d) % NX for d in range(NX)]
        self.along_x = [self.z * NX + to for to in self.next_x]
        self.low, self.high = pl.ds(0, self.nz // 2), pl.ds(self.nz // 2, self.nz // 2)
        self.next_z = [(self.z + d) % self.nz for d in range(self.nz)]
        self.along_z = [to * NX + self.x for to in self.next_z]
        self.next_r = [(self.r + d) % self.rows for d in range(self.rows)]
        self.sends = []

    def go(self, copy, only=None):
        copy.start()
        tracked = Copy(copy, only)
        self.sends.append(tracked)
        return tracked

    def start(self, copies, only=None):
        return [self.go(copy, only) for copy in copies]

    def to_all_x(self, src, dst, sems):
        send, recv = sems
        return [
            remote(src(self.next_x[d]), dst(d), send.at[d], recv.at[d], self.r, self.along_x[d]) for d in (1, 3, 2)
        ]

    def to_all_z(self, src, dst, sems):
        send, recv = sems
        order = [4, 3, 5, 2, 6, 1, 7] if self.nz == 8 else range(1, self.nz)
        return [
            remote(src(self.next_z[d]), dst(d), send.at[d], recv.at[d], self.r, self.along_z[d]) for d in order
        ]


def landed(copies):
    for copy in copies:
        copy.wait_recv()


class Reduce:
    def __init__(self, at, buffers, x_sems, z_sems):
        self.at = at
        self.parts, self.from_a, self.from_b, self.from_l, self.from_r, self.part_sum, self.from_z = buffers
        self.x_send, self.x_recv = x_sems
        self.z_sems = z_sems
        self.copies = {}

    def send_x(self, kind, src, dst, d):
        at = self.at
        copy = remote(src, dst, self.x_send.at[kind], self.x_recv.at[kind], at.r, at.along_x[d])
        self.copies[kind] = at.go(copy)

    def first(self):
        at = self.at
        left, right, far = at.next_x[3], at.next_x[1], at.next_x[2]
        self.send_x(0, self.parts.at[far, at.low], self.from_a, 1)
        self.send_x(1, self.parts.at[far, at.high], self.from_b, 3)
        self.send_x(2, self.parts.at[right, at.high], self.from_l.at[at.high], 1)
        self.send_x(3, self.parts.at[left, at.low], self.from_r.at[at.low], 3)

    def second(self):
        at = self.at
        left, right = at.next_x[3], at.next_x[1]
        self.copies[0].wait_recv()
        own = self.parts[right, at.low].astype(F32)
        self.parts[right, at.low] = (own + self.from_a[...].astype(F32)).astype(BF16)
        self.send_x(4, self.parts.at[right, at.low], self.from_l.at[at.low], 1)
        self.copies[1].wait_recv()
        own = self.parts[left, at.high].astype(F32)
        self.parts[left, at.high] = (own + self.from_b[...].astype(F32)).astype(BF16)
        self.send_x(5, self.parts.at[left, at.high], self.from_r.at[at.high], 3)

    def third(self):
        at = self.at
        for kind in range(2, 6):
            self.copies[kind].wait_recv()

        def one(i, carry):
            total = self.parts[at.x, i].astype(F32) + self.from_l[i].astype(F32) + self.from_r[i].astype(F32)
            self.part_sum[i] = total.astype(BF16)
            return carry

        lax.fori_loop(0, at.nz, one, 0)
        self.send_z()

    def send_z(self):
        at = self.at
        self.z_copies = at.start(
            at.to_all_z(lambda to: self.part_sum.at[to], lambda d: self.from_z.at[d], self.z_sems)
        )

    def result(self):
        at = self.at
        landed(self.z_copies)
        total = self.part_sum[at.z].astype(F32)
        for d in range(1, at.nz):
            total = total + self.from_z[d].astype(F32)
        return total


class ReduceDirect(Reduce):
    def __init__(self, at, buffers, x_sems, z_sems):
        self.at = at
        self.parts, self.from_x, self.part_sum, self.from_z = buffers
        self.x_sems, self.z_sems = x_sems, z_sems

    def first(self):
        at = self.at
        self.x_copies = at.start(
            at.to_all_x(lambda to: self.parts.at[to], lambda d: self.from_x.at[d - 1], self.x_sems)
        )

    def second(self):
        at = self.at
        landed(self.x_copies)

        def one(i, carry):
            total = self.parts[at.x, i].astype(F32)
            for d in range(NX - 1):
                total = total + self.from_x[d, i].astype(F32)
            self.part_sum[i] = total.astype(BF16)
            return carry

        lax.fori_loop(0, at.nz, one, 0)
        self.send_z()


class Gather:
    def __init__(self, at, whole, x_sems, z_sems, only=None):
        self.at, self.whole, self.only = at, whole, only
        self.z_made = at.to_all_z(lambda to: whole.at[at.z, at.x], lambda d: whole.at[at.z, at.x], z_sems)
        self.x_made = at.to_all_x(lambda to: whole.at[:, at.x], lambda d: whole.at[:, at.x], x_sems)

    def first(self):
        self.z_copies = self.at.start(self.z_made, self.only)

    def second(self):
        landed(self.z_copies)
        self.x_copies = self.at.start(self.x_made, self.only)

    def wait(self):
        landed(self.x_copies)


class Flow:
    def __init__(self, at, buffers, sems, separate):
        self.at, self.separate = at, separate
        self.source, self.block, self.parts, self.from_z, self.steps, self.lead, self.out, self.whole = buffers
        self.sems = sems

    def feed(self):
        at = self.at
        self.block[at.x] = self.source[at.x]
        self.fed = at.start(
            at.to_all_x(lambda to: self.source.at[to], lambda d: self.block.at[at.x], self.sems[0])
        )

    def right(self, factors, positions, rank):
        at = self.at
        landed(self.fed)
        count, thin, sides = self.block.shape
        product = dot(factors[...].reshape(count * thin, -1), self.block[...].reshape(count * thin, sides), TN)
        self.parts[:, :rank] = product[: positions * rank].astype(BF16).reshape(positions, rank, sides)
        lead = product[positions * rank :]
        chunks = (NX - 1) * rank // CHUNK
        for i in range(at.nz):
            part = lead[i * CHUNK : (i + 1) * CHUNK] if i < chunks else jnp.zeros((CHUNK, sides), F32)
            self.parts[i, rank:] = part.astype(BF16)
        self.z_copies = at.start(
            at.to_all_z(lambda to: self.parts.at[to], lambda d: self.from_z.at[d], self.sems[1])
        )

    def share(self, rank, off):
        at = self.at
        landed(self.z_copies)
        total = self.parts[at.z].astype(F32)
        for d in range(1, at.nz):
            total = total + self.from_z[d].astype(F32)
        self.steps[at.x] = jnp.where(off, 0.0, total[:rank]).astype(BF16)
        self.lead[at.x, at.z] = total[rank:].astype(BF16)
        self.x_copies = at.start(
            at.to_all_x(lambda to: self.steps.at[at.x], lambda d: self.steps.at[at.x], self.sems[2])
        )
        own = self.lead.at[at.x, at.z]
        self.lead_z = at.start(at.to_all_z(lambda to: own, lambda d: own, self.sems[3]))

    def left(self, factors):
        at = self.at
        landed(self.x_copies)
        nz, thin, width = factors.shape
        rows = factors[...].reshape(nz * thin, width)
        rank = self.steps.shape[1]
        if self.separate:
            for m in range(1, NX):
                lanes = lanes_of(m)
                product = dot(rows[:, m * rank : (m + 1) * rank], self.steps[m, :, : lanes.stop - lanes.start])
                self.out[:, :, lanes] = product.astype(BF16).reshape(nz, thin, -1)
        else:
            product = dot(rows, self.steps[...].reshape(width, -1))
            self.out[...] = product.astype(BF16).reshape(nz, thin, -1)
        self.whole[at.z] = self.out[at.z]
        self.out_copies = at.start(
            at.to_all_z(lambda to: self.out.at[to], lambda d: self.whole.at[at.z], self.sems[4])
        )

    def lead_x(self):
        at = self.at
        landed(self.lead_z)
        own = self.lead.at[at.x]
        self.lead_copies = at.start(at.to_all_x(lambda to: own, lambda d: own, self.sems[5]))

    def lead_rows(self, k, m):
        rank = self.steps.shape[1]
        pieces = rank // CHUNK
        first = (k - 1) * pieces
        return jnp.concatenate([self.lead[m, first + i].astype(F32) for i in range(pieces)], axis=0)


def lanes_of(m):
    first = (None, 0, LANES, 2 * LANES)[m]
    return slice(first, first + (LANES if m < 3 else 2 * LANES))


def take(refs, count):
    return [refs.pop(0) for _ in range(count)]


def kernel(sides_in, left_in, right_in, known_in, dleft_in, dright_in, inverse_in, updated, solved, *scratch):
    at = Place()
    r, c, go = at.r, at.c, at.go
    refs = list(scratch)
    left, right, known, coeff, sides_raw, sides, dleft_raw, dright_raw, dleft, inverse = take(refs, 10)
    packs, lead_left, base_whole, factors, own_factors, own_left = take(refs, 6)
    wide, lead_coeff = take(refs, 2)
    lead_buffers = take(refs, 4)
    bulk_buffers = [take(refs, 7) for _ in GROUPS[1:]]
    flow_buffers = [take(refs, 8) for _ in range(2)]
    start = flow_buffers[1][0]
    load_sem, gather_send, gather_recv, bulk_send, bulk_recv = take(refs, 5)
    x_send, x_recv, z_send, z_recv = take(refs, 4)
    pack_send, pack_recv, start_send, start_recv = take(refs, 4)
    x_sems = [(x_send.at[i], x_recv.at[i]) for i in range(x_send.shape[0])]
    z_sems = [(z_send.at[i], z_recv.at[i]) for i in range(z_send.shape[0])]

    depth, priors = known_in.shape[1], known_in.shape[0]
    local_rows, steps, thin, rank = dleft_in.shape
    sides_count = sides.shape[2]
    tile = left.shape[3]
    width = steps * rank
    half = packs.shape[2] // 2

    prior = [ReduceDirect(at, lead_buffers, x_sems.pop(), z_sems.pop())]
    for i, buffers in enumerate(bulk_buffers):
        prior.append(Reduce(at, buffers, (bulk_send.at[i], bulk_recv.at[i]), z_sems.pop()))
    lead_all = Gather(at, lead_left, x_sems.pop(), z_sems.pop())
    base_all = Gather(at, base_whole, x_sems.pop(), z_sems.pop(), r < steps)
    flows = [
        Flow(
            at,
            buffers,
            (x_sems.pop(), z_sems.pop(), x_sems.pop(), z_sems.pop(), z_sems.pop(), x_sems.pop()),
            separate,
        )
        for buffers, separate in zip(flow_buffers, (True, False))
    ]
    cross, near = flows
    factor_copies = at.to_all_x(lambda to: factors.at[to], lambda d: own_factors.at[at.x], x_sems.pop())
    left_copies = at.to_all_z(lambda to: dleft.at[to], lambda d: own_left.at[at.z], z_sems.pop())

    loads = [
        pltpu.make_async_copy(src, dst, load_sem.at[i])
        for i, (src, dst) in enumerate(
            (
                (known_in, known.at[:, pl.ds(r * depth, depth)]),
                (dleft_in, dleft_raw),
                (dright_in, dright_raw),
                (right_in, right),
                (left_in, left),
                (inverse_in, inverse),
                (sides_in, sides_raw),
            )
        )
    ]
    for load in loads:
        load.start()
    barrier = pltpu.get_barrier_semaphore()
    peers = [(at.next_r[d], c) for d in range(1, at.rows)]
    peers += [(r, at.along_x[d]) for d in range(1, NX)]
    peers += [(r, at.along_z[d]) for d in range(1, at.nz)]
    for row, col in peers:
        pl.semaphore_signal(barrier, inc=1, device_id={ROW: row, COL: col}, device_id_type=MESH)

    for load in loads[1:3]:
        load.wait()
    factors[...] = jnp.zeros(factors.shape, BF16)
    packs[r] = jnp.zeros(packs.shape[1:], BF16)
    for m in range(steps):
        lanes = slice(m * rank, (m + 1) * rank)
        packs[r, :, lanes] = dleft_raw[0, m]
        packs[r, :, half + m * rank : half + (m + 1) * rank] = dright_raw[0, m]
        for a in range(local_rows):
            dleft[a, :, lanes] = dleft_raw[a, m]
            factors[m, :, a * rank : (a + 1) * rank] = dright_raw[a, m]
    loads[0].wait()
    pl.semaphore_wait(barrier, len(peers))

    def block(row, j):
        return known.at[j, pl.ds(row * depth, depth)]

    def share(row_of_block, j, kind, target):
        part = block(row_of_block, j)
        return remote(part, part, gather_send.at[kind, j], gather_recv.at[kind, j], target, c)

    own_up, own_down, relay, over = [], [], [], [[], [], [], []]
    for j in range(priors):
        own_up.append(go(share(r, j, 0, at.up)))
        own_down.append(go(share(r, j, 1, at.down)))
        over[0].append(go(share(r, j, 3, at.partner)))
    left_copies = at.start(left_copies)
    own_left[at.z] = dleft[at.z]
    for j in range(priors):
        own_up[j].wait_recv()
        over[1].append(go(share(at.down, j, 4, at.partner)))
        if j < priors // 2:
            relay.append(go(share(at.down, j, 2, at.up)))
        own_down[j].wait_recv()
        over[2].append(go(share(at.up, j, 5, at.partner)))
        if j >= priors // 2:
            relay.append(go(share(at.up, j, 2, at.down)))

    sends_pack = jnp.logical_and(r > 0, r < steps)
    pack_copies = [
        remote(packs.at[r], packs.at[r], pack_send.at[d], pack_recv.at[r], at.next_r[d], c)
        for d in range(1, at.rows)
    ]

    @pl.when(sends_pack)
    def _():
        for copy in pack_copies:
            copy.start()

    loads[6].wait()
    whole_sides = sides_raw[...].astype(F32)
    for a in range(local_rows):
        sides[a] = whole_sides[:, a]

    for load in loads[3:6]:
        load.wait()
    for j in range(priors):
        relay[j].wait_recv()
        over[3].append(go(share(at.far, j, 6, at.partner)))
        for kind in range(4):
            over[kind][j].wait_recv()
        product = dot(right[:, j].reshape(-1, tile), known[j])
        coeff[:, pl.ds(j * rank, rank)] = product.astype(BF16).reshape(local_rows, rank, sides_count)

    def multiply(g):
        first = GROUPS[g][0]

        def one(i, carry):
            term = dot(left[i + first].reshape(priors * rank, tile), coeff[i + first], TN)
            term = term.astype(BF16).reshape(at.nz, NX, thin, sides_count)
            for at_x in range(NX):
                prior[g].parts[at_x, :, i] = term[:, at_x]
            return carry

        lax.fori_loop(0, len(GROUPS[g]), one, 0)

    def own_base(g):
        total = prior[g].result()
        for i, a in enumerate(GROUPS[g]):
            updated[a] = sides[a] - total[i]

    multiply(0)
    prior[0].first()

    for k in range(1, steps):

        @pl.when(r != k)
        def _():
            remote(packs.at[k], packs.at[k], pack_send.at[1], pack_recv.at[k], at.next_r[1], c).wait_recv()

    lead_left[at.z, at.x] = jnp.zeros(lead_left.shape[2:], BF16)
    for k in range(1, steps):
        lanes = lanes_of(k)
        lead_left[at.z, at.x, :, lanes.start : lanes.start + k * rank] = packs[k, :, : k * rank]
        for m in range(steps):
            first = (local_rows + k - 1) * rank
            factors[m, :, first : first + rank] = packs[k, :, half + m * rank : half + (m + 1) * rank]
    lead_all.first()
    factor_copies = at.start(factor_copies)
    own_factors[at.x] = factors[at.x]
    multiply(1)
    prior[0].second()
    lead_all.second()
    multiply(2)
    own_base(0)

    @pl.when(r < steps)
    def _():
        base_whole[at.z, at.x] = updated[0].astype(BF16)
        base_all.first()

    lead_all.wait()
    whole_left = lead_left[...].reshape(tile, lead_left.shape[3])
    cross.source[...] = jnp.zeros(cross.source.shape, BF16)
    for m in range(1, steps):
        lanes = lanes_of(m)
        product = dot(inverse[m], whole_left[:, lanes]).astype(BF16)
        wide[:, lanes] = product
        cross.source[m, :, : lanes.stop - lanes.start] = product
    cross.feed()

    @pl.when(r < steps)
    def _():
        base_all.second()

    start_copies = [
        remote(start.at[r], start.at[r], start_send.at[d], start_recv.at[r], at.next_r[d], c)
        for d in range(1, at.rows)
    ]
    landed(factor_copies)
    cross.right(own_factors, local_rows, rank)

    @pl.when(r < steps)
    def _():
        base_all.wait()
        start[r] = dot(inverse[r], base_whole[...].reshape(tile, sides_count)).astype(BF16)
        for copy in start_copies:
            copy.start()

    prior[1].first()
    off = jnp.logical_and(at.z == 0, r <= at.x)
    cross.share(rank, off)
    for k in range(steps):

        @pl.when(r != k)
        def _():
            remote(start.at[k], start.at[k], start_send.at[1], start_recv.at[k], at.next_r[1], c).wait_recv()

    near.feed()
    prior[1].second()
    near.right(own_factors, local_rows, rank)
    prior[2].first()
    landed(left_copies)
    cross.left(own_left)
    cross.lead_x()
    prior[1].third()
    near.share(rank, off)
    prior[2].second()
    near.left(own_left)
    near.lead_x()
    own_base(1)
    prior[2].third()
    landed(cross.lead_copies)
    landed(cross.out_copies)
    landed(near.lead_copies)

    lead_coeff[...] = jnp.zeros(lead_coeff.shape, BF16)
    for m in range(steps - 1):
        for k in range(m + 1, steps):
            value = near.lead_rows(k, m)
            if m:
                lanes = lanes_of(m)
                size = lanes.stop - lanes.start
                value = value - dot(cross.lead_rows(k, m).astype(BF16)[:, :size], lead_coeff[lanes])
            first = lanes_of(k).start + m * rank
            lead_coeff[first : first + rank] = value.astype(BF16)
    for m in range(steps):
        answer = start[m].astype(F32)
        if m:
            answer = answer - dot(wide[:, lanes_of(m)], lead_coeff[lanes_of(m)])
        solved[m] = answer.astype(BF16)
    correction = dot(cross.whole[...].reshape(local_rows * thin, -1), lead_coeff[...])
    correction = correction.reshape(local_rows, thin, sides_count)
    own_base(2)
    landed(near.out_copies)
    for a in range(local_rows):
        updated[a] = updated[a] + (correction[a] - near.whole[a].astype(F32))

    for copy in at.sends:
        copy.close()

    @pl.when(sends_pack)
    def _():
        for copy in pack_copies:
            copy.wait_send()

    @pl.when(r < steps)
    def _():
        for copy in start_copies:
            copy.wait_send()


def local(right_sides, prior_left, prior_right, solved_prior, diag_left, diag_right, diag_inverse):
    thin, local_rows, sides = right_sides.shape
    priors, rank, tile = prior_left.shape[1:]
    diag_left, diag_right = jnp.swapaxes(diag_left, 2, 3), jnp.swapaxes(diag_right, 2, 3)
    steps = diag_left.shape[1]
    rows, cols = lax.axis_size(ROW), lax.axis_size(COL)
    nz = cols // NX
    width = steps * rank
    block = rank + CHUNK
    factor_width = (local_rows + NX - 1) * rank

    shapes = [
        prior_left.shape,
        prior_right.shape,
        (priors, tile, sides),
        (local_rows, priors * rank, sides),
        right_sides.shape,
        ((local_rows, thin, sides), F32),
        diag_left.shape,
        diag_right.shape,
        (local_rows, thin, width),
        diag_inverse.shape,
        (rows, thin, 4 * LANES),
        (nz, NX, thin, 4 * LANES),
        (nz, NX, thin, sides),
        (steps, thin, factor_width),
        (NX, thin, factor_width),
        (nz, thin, width),
        (thin, 4 * LANES),
        (4 * LANES, sides),
    ]
    one = (len(GROUPS[0]), thin, sides)
    shapes += [(NX, nz, *one), (NX - 1, nz, *one), (nz, *one), (nz, *one)]
    for group in GROUPS[1:]:
        for lead in ((NX, nz), (nz // 2,), (nz // 2,), (nz,), (nz,), (nz,), (nz,)):
            shapes.append((*lead, len(group), thin, sides))
    for out in (4 * LANES, sides):
        shapes += [
            (steps, thin, sides),
            (NX, thin, sides),
            (nz, block, sides),
            (nz, block, sides),
            (NX, rank, sides),
            (NX, nz, CHUNK, sides),
            (nz, thin, out),
            (nz, thin, out),
        ]
    scratch = [pltpu.VMEM(*shape) if isinstance(shape[0], tuple) else pltpu.VMEM(shape, BF16) for shape in shapes]
    bulk = len(GROUPS) - 1
    for shape in (
        (7,),
        (7, priors),
        (7, priors),
        (bulk, 6),
        (bulk, 6),
        (10, NX),
        (10, NX),
        (12, nz),
        (12, nz),
        (rows,),
        (steps,),
        (rows,),
        (steps,),
    ):
        scratch.append(pltpu.SemaphoreType.DMA(shape))
    updated, solved = pl.pallas_call(
        kernel,
        out_shape=(
            jax.ShapeDtypeStruct((local_rows, thin, sides), F32),
            jax.ShapeDtypeStruct((steps, thin, sides), BF16),
        ),
        in_specs=[pl.BlockSpec(memory_space=pl.ANY)] * 7,
        out_specs=(pl.BlockSpec(memory_space=pltpu.VMEM), pl.BlockSpec(memory_space=pltpu.VMEM)),
        scratch_shapes=scratch,
        compiler_params=pltpu.CompilerParams(
            collective_id=0, has_side_effects=True, vmem_limit_bytes=56 * 1024 * 1024
        ),
    )(right_sides, prior_left, prior_right, solved_prior, diag_left, diag_right, diag_inverse)
    return jnp.swapaxes(updated, 0, 1), solved


def solution(mesh):
    return jax.shard_map(
        local,
        mesh=mesh,
        in_specs=(
            P(COL, ROW, None),
            P(ROW, COL, None, None),
            P(ROW, COL, None, None),
            P(COL, ROW, None),
            P(ROW, None, None, COL),
            P(ROW, None, None, COL),
            P(None, COL, None),
        ),
        out_specs=(P(COL, ROW, None), P(None, COL, None)),
        check_vma=False,
    )
```

```python
import jax
import jax.numpy as jnp
from jax import lax
from jax.experimental import pallas as pl
from jax.experimental.pallas import tpu as pltpu
from jax.sharding import PartitionSpec as P

ROW = "row"
COL = "col"
CORES = 2
NX = 4
MESH = pl.DeviceIdType.MESH
F32 = jnp.float32
BF16 = jnp.bfloat16
LANES = 128
GROUPS = ((0,), (1, 2), (3, 4), (5, 6, 7))
CHUNK = 24
TN = (((0,), (0,)), ((), ()))


def dot(a, b, dims=None):
    if dims is None:
        return jnp.dot(a, b, preferred_element_type=F32)
    return lax.dot_general(a, b, dims, preferred_element_type=F32)


def remote(src, dst, send, recv, row, col):
    return pltpu.make_async_remote_copy(
        src_ref=src,
        dst_ref=dst,
        send_sem=send,
        recv_sem=recv,
        device_id={ROW: row, COL: col},
        device_id_type=MESH,
    )


class Copy:
    def __init__(self, copy, only=None):
        self.copy, self.only, self.landed = copy, only, False

    def wait_recv(self):
        self.copy.wait_recv()
        self.landed = True

    def close(self):
        def rest():
            if not self.landed:
                self.copy.wait_recv()
            self.copy.wait_send()

        if self.only is None:
            rest()
        else:
            pl.when(self.only)(rest)


class Place:
    def __init__(self):
        self.rows, self.cols = lax.axis_size(ROW), lax.axis_size(COL)
        self.ny, self.nz = self.rows // CORES, self.cols // NX
        self.r, self.c = lax.axis_index(ROW), lax.axis_index(COL)
        self.y, self.q = self.r // CORES, self.r % CORES
        self.z, self.x = self.c // NX, self.c % NX
        self.up, self.down, self.far = (((self.y + d) % self.ny) * CORES + self.q for d in (1, self.ny - 1, 2))
        self.partner = self.y * CORES + 1 - self.q
        self.next_x = [(self.x + d) % NX for d in range(NX)]
        self.along_x = [self.z * NX + to for to in self.next_x]
        self.low, self.high = pl.ds(0, self.nz // 2), pl.ds(self.nz // 2, self.nz // 2)
        self.next_z = [(self.z + d) % self.nz for d in range(self.nz)]
        self.along_z = [to * NX + self.x for to in self.next_z]
        self.next_r = [(self.r + d) % self.rows for d in range(self.rows)]
        self.sends = []

    def go(self, copy, only=None):
        copy.start()
        tracked = Copy(copy, only)
        self.sends.append(tracked)
        return tracked

    def start(self, copies, only=None):
        return [self.go(copy, only) for copy in copies]

    def to_all_x(self, src, dst, sems):
        send, recv = sems
        return [
            remote(src(self.next_x[d]), dst(d), send.at[d], recv.at[d], self.r, self.along_x[d]) for d in (1, 3, 2)
        ]

    def to_all_z(self, src, dst, sems):
        send, recv = sems
        order = [4, 3, 5, 2, 6, 1, 7] if self.nz == 8 else range(1, self.nz)
        return [
            remote(src(self.next_z[d]), dst(d), send.at[d], recv.at[d], self.r, self.along_z[d]) for d in order
        ]


def landed(copies):
    for copy in copies:
        copy.wait_recv()


class Reduce:
    def __init__(self, at, buffers, x_sems, z_sems):
        self.at = at
        self.parts, self.from_a, self.from_b, self.from_l, self.from_r, self.part_sum, self.from_z = buffers
        self.x_send, self.x_recv = x_sems
        self.z_sems = z_sems
        self.copies = {}

    def send_x(self, kind, src, dst, d):
        at = self.at
        copy = remote(src, dst, self.x_send.at[kind], self.x_recv.at[kind], at.r, at.along_x[d])
        self.copies[kind] = at.go(copy)

    def first(self):
        at = self.at
        left, right, far = at.next_x[3], at.next_x[1], at.next_x[2]
        self.send_x(0, self.parts.at[far, at.low], self.from_a, 1)
        self.send_x(1, self.parts.at[far, at.high], self.from_b, 3)
        self.send_x(2, self.parts.at[right, at.high], self.from_l.at[at.high], 1)
        self.send_x(3, self.parts.at[left, at.low], self.from_r.at[at.low], 3)

    def second(self):
        at = self.at
        left, right = at.next_x[3], at.next_x[1]
        self.copies[0].wait_recv()
        own = self.parts[right, at.low].astype(F32)
        self.parts[right, at.low] = (own + self.from_a[...].astype(F32)).astype(BF16)
        self.send_x(4, self.parts.at[right, at.low], self.from_l.at[at.low], 1)
        self.copies[1].wait_recv()
        own = self.parts[left, at.high].astype(F32)
        self.parts[left, at.high] = (own + self.from_b[...].astype(F32)).astype(BF16)
        self.send_x(5, self.parts.at[left, at.high], self.from_r.at[at.high], 3)

    def third(self):
        at = self.at
        for kind in range(2, 6):
            self.copies[kind].wait_recv()

        def one(i, carry):
            total = self.parts[at.x, i].astype(F32) + self.from_l[i].astype(F32) + self.from_r[i].astype(F32)
            self.part_sum[i] = total.astype(BF16)
            return carry

        lax.fori_loop(0, at.nz, one, 0)
        self.send_z()

    def send_z(self):
        at = self.at
        self.z_copies = at.start(
            at.to_all_z(lambda to: self.part_sum.at[to], lambda d: self.from_z.at[d], self.z_sems)
        )

    def result(self):
        at = self.at
        landed(self.z_copies)
        total = self.part_sum[at.z].astype(F32)
        for d in range(1, at.nz):
            total = total + self.from_z[d].astype(F32)
        return total


class ReduceDirect(Reduce):
    def __init__(self, at, buffers, x_sems, z_sems):
        self.at = at
        self.parts, self.from_x, self.part_sum, self.from_z = buffers
        self.x_sems, self.z_sems = x_sems, z_sems

    def first(self):
        at = self.at
        self.x_copies = at.start(
            at.to_all_x(lambda to: self.parts.at[to], lambda d: self.from_x.at[d - 1], self.x_sems)
        )

    def second(self):
        at = self.at
        landed(self.x_copies)

        def one(i, carry):
            total = self.parts[at.x, i].astype(F32)
            for d in range(NX - 1):
                total = total + self.from_x[d, i].astype(F32)
            self.part_sum[i] = total.astype(BF16)
            return carry

        lax.fori_loop(0, at.nz, one, 0)
        self.send_z()


class Gather:
    def __init__(self, at, whole, x_sems, z_sems, only=None):
        self.at, self.whole, self.only = at, whole, only
        self.z_made = at.to_all_z(lambda to: whole.at[at.z, at.x], lambda d: whole.at[at.z, at.x], z_sems)
        self.x_made = at.to_all_x(lambda to: whole.at[:, at.x], lambda d: whole.at[:, at.x], x_sems)

    def first(self):
        self.z_copies = self.at.start(self.z_made, self.only)

    def second(self):
        landed(self.z_copies)
        self.x_copies = self.at.start(self.x_made, self.only)

    def wait(self):
        landed(self.x_copies)


class Flow:
    def __init__(self, at, buffers, sems, separate):
        self.at, self.separate = at, separate
        self.source, self.block, self.parts, self.from_z, self.steps, self.lead, self.out, self.whole = buffers
        self.sems = sems

    def feed(self):
        at = self.at
        self.block[at.x] = self.source[at.x]
        self.fed = at.start(
            at.to_all_x(lambda to: self.source.at[to], lambda d: self.block.at[at.x], self.sems[0])
        )

    def right(self, factors, positions, rank):
        at = self.at
        landed(self.fed)
        count, thin, sides = self.block.shape
        product = dot(factors[...].reshape(count * thin, -1), self.block[...].reshape(count * thin, sides), TN)
        self.parts[:, :rank] = product[: positions * rank].astype(BF16).reshape(positions, rank, sides)
        lead = product[positions * rank :]
        chunks = (NX - 1) * rank // CHUNK
        for i in range(at.nz):
            part = lead[i * CHUNK : (i + 1) * CHUNK] if i < chunks else jnp.zeros((CHUNK, sides), F32)
            self.parts[i, rank:] = part.astype(BF16)
        self.z_copies = at.start(
            at.to_all_z(lambda to: self.parts.at[to], lambda d: self.from_z.at[d], self.sems[1])
        )

    def share(self, rank, off):
        at = self.at
        landed(self.z_copies)
        total = self.parts[at.z].astype(F32)
        for d in range(1, at.nz):
            total = total + self.from_z[d].astype(F32)
        self.steps[at.x] = jnp.where(off, 0.0, total[:rank]).astype(BF16)
        self.lead[at.x, at.z] = total[rank:].astype(BF16)
        self.x_copies = at.start(
            at.to_all_x(lambda to: self.steps.at[at.x], lambda d: self.steps.at[at.x], self.sems[2])
        )
        own = self.lead.at[at.x, at.z]
        self.lead_z = at.start(at.to_all_z(lambda to: own, lambda d: own, self.sems[3]))

    def left(self, factors):
        at = self.at
        landed(self.x_copies)
        nz, thin, width = factors.shape
        rows = factors[...].reshape(nz * thin, width)
        rank = self.steps.shape[1]
        if self.separate:
            for m in range(1, NX):
                lanes = lanes_of(m)
                product = dot(rows[:, m * rank : (m + 1) * rank], self.steps[m, :, : lanes.stop - lanes.start])
                self.out[:, :, lanes] = product.astype(BF16).reshape(nz, thin, -1)
        else:
            product = dot(rows, self.steps[...].reshape(width, -1))
            self.out[...] = product.astype(BF16).reshape(nz, thin, -1)
        self.whole[at.z] = self.out[at.z]
        self.out_copies = at.start(
            at.to_all_z(lambda to: self.out.at[to], lambda d: self.whole.at[at.z], self.sems[4])
        )

    def lead_x(self):
        at = self.at
        landed(self.lead_z)
        own = self.lead.at[at.x]
        self.lead_copies = at.start(at.to_all_x(lambda to: own, lambda d: own, self.sems[5]))

    def lead_rows(self, k, m):
        rank = self.steps.shape[1]
        pieces = rank // CHUNK
        first = (k - 1) * pieces
        return jnp.concatenate([self.lead[m, first + i].astype(F32) for i in range(pieces)], axis=0)


def lanes_of(m):
    first = (None, 0, LANES, 2 * LANES)[m]
    return slice(first, first + (LANES if m < 3 else 2 * LANES))


def take(refs, count):
    return [refs.pop(0) for _ in range(count)]


def kernel(sides_in, left_in, right_in, known_in, dleft_in, dright_in, inverse_in, updated, solved, *scratch):
    at = Place()
    r, c, go = at.r, at.c, at.go
    refs = list(scratch)
    left, right, known, coeff, sides_raw, sides, dleft_raw, dright_raw, dleft, inverse = take(refs, 10)
    packs, lead_left, factors, own_factors, own_left = take(refs, 5)
    base_block, columns, start_parts, start_from = take(refs, 4)
    wide, lead_coeff = take(refs, 2)
    lead_buffers = take(refs, 4)
    bulk_buffers = [take(refs, 7) for _ in GROUPS[1:]]
    flow_buffers = [take(refs, 8) for _ in range(2)]
    start = flow_buffers[1][0]
    load_sem, gather_send, gather_recv, bulk_send, bulk_recv = take(refs, 5)
    x_send, x_recv, z_send, z_recv = take(refs, 4)
    pack_send, pack_recv, start_send, start_recv = take(refs, 4)
    x_sems = [(x_send.at[i], x_recv.at[i]) for i in range(x_send.shape[0])]
    z_sems = [(z_send.at[i], z_recv.at[i]) for i in range(z_send.shape[0])]

    depth, priors = known_in.shape[1], known_in.shape[0]
    local_rows, steps, thin, rank = dleft_in.shape
    sides_count = sides.shape[2]
    tile = left.shape[3]
    width = steps * rank
    half = packs.shape[2] // 2
    solving = r < steps
    below = jnp.logical_and(r > 0, solving)

    prior = [ReduceDirect(at, lead_buffers, x_sems.pop(), z_sems.pop())]
    for i, buffers in enumerate(bulk_buffers):
        prior.append(Reduce(at, buffers, (bulk_send.at[i], bulk_recv.at[i]), z_sems.pop()))
    lead_all = Gather(at, lead_left, x_sems.pop(), z_sems.pop(), below)
    base_copies = at.to_all_x(lambda to: base_block.at[at.x], lambda d: base_block.at[at.x], x_sems.pop())
    start_z_copies = at.to_all_z(lambda to: start_parts.at[to], lambda d: start_from.at[d], z_sems.pop())
    column_copies = at.to_all_z(
        lambda to: inverse.at[r % steps, :, pl.ds(pl.multiple_of(to * LANES, LANES), LANES)],
        lambda d: columns.at[at.z],
        z_sems.pop(),
    )
    start_copies = [
        remote(start.at[r % steps], start.at[r % steps], start_send.at[d], start_recv.at[r % steps], at.next_r[d], c)
        for d in range(1, at.rows)
    ]
    pack_copies = [
        remote(packs.at[r], packs.at[r], pack_send.at[d], pack_recv.at[r % steps], at.next_r[d], c)
        for d in range(1, at.rows)
    ]
    running = {}
    flows = [
        Flow(
            at,
            buffers,
            (x_sems.pop(), z_sems.pop(), x_sems.pop(), z_sems.pop(), z_sems.pop(), x_sems.pop()),
            separate,
        )
        for buffers, separate in zip(flow_buffers, (True, False))
    ]
    cross, near = flows
    factor_copies = at.to_all_x(lambda to: factors.at[to], lambda d: own_factors.at[at.x], x_sems.pop())
    left_copies = at.to_all_z(lambda to: dleft.at[to], lambda d: own_left.at[at.z], z_sems.pop())

    loads = [
        pltpu.make_async_copy(src, dst, load_sem.at[i])
        for i, (src, dst) in enumerate(
            (
                (known_in, known.at[:, pl.ds(r * depth, depth)]),
                (dleft_in, dleft_raw),
                (dright_in, dright_raw),
                (inverse_in, inverse),
                (right_in, right),
                (left_in, left),
                (sides_in, sides_raw),
            )
        )
    ]
    for load in loads:
        load.start()
    barrier = pltpu.get_barrier_semaphore()
    peers = [(at.next_r[d], c) for d in range(1, at.rows)]
    peers += [(r, at.along_x[d]) for d in range(1, NX)]
    peers += [(r, at.along_z[d]) for d in range(1, at.nz)]
    for row, col in peers:
        pl.semaphore_signal(barrier, inc=1, device_id={ROW: row, COL: col}, device_id_type=MESH)

    for load in loads[1:3]:
        load.wait()
    factors[...] = jnp.zeros(factors.shape, BF16)
    packs[r] = jnp.zeros(packs.shape[1:], BF16)
    for m in range(steps):
        lanes = slice(m * rank, (m + 1) * rank)
        packs[r, :, half + m * rank : half + (m + 1) * rank] = dright_raw[0, m]
        for a in range(local_rows):
            dleft[a, :, lanes] = dleft_raw[a, m]
            factors[m, :, a * rank : (a + 1) * rank] = dright_raw[a, m]
    lead_left[at.z, at.x] = jnp.zeros(lead_left.shape[2:], BF16)
    for m in range(steps - 1):
        lead_left[at.z, at.x, :, m * rank : (m + 1) * rank] = dleft_raw[0, m]
    loads[0].wait()
    pl.semaphore_wait(barrier, len(peers))

    def block(row, j):
        return known.at[j, pl.ds(row * depth, depth)]

    def share(row_of_block, j, kind, target):
        part = block(row_of_block, j)
        return remote(part, part, gather_send.at[kind, j], gather_recv.at[kind, j], target, c)

    own_up, own_down, relay, over = [], [], [], [[], [], [], []]
    for j in range(priors):
        own_up.append(go(share(r, j, 0, at.up)))
        own_down.append(go(share(r, j, 1, at.down)))
        over[0].append(go(share(r, j, 3, at.partner)))
    @pl.when(below)
    def _():
        lead_all.first()

    loads[3].wait()

    @pl.when(solving)
    def _():
        running["columns"] = at.start(column_copies, solving)
        columns[at.z] = inverse[r % steps, :, pl.ds(pl.multiple_of(at.z * LANES, LANES), LANES)]

    left_copies = at.start(left_copies)
    own_left[at.z] = dleft[at.z]
    for j in range(priors):
        own_up[j].wait_recv()
        over[1].append(go(share(at.down, j, 4, at.partner)))
        if j < priors // 2:
            relay.append(go(share(at.down, j, 2, at.up)))
        own_down[j].wait_recv()
        over[2].append(go(share(at.up, j, 5, at.partner)))
        if j >= priors // 2:
            relay.append(go(share(at.up, j, 2, at.down)))

    @pl.when(below)
    def _():
        lead_all.second()

    loads[6].wait()
    whole_sides = sides_raw[...].astype(F32)
    for a in range(local_rows):
        sides[a] = whole_sides[:, a]

    for load in loads[4:6]:
        load.wait()
    for j in range(priors):
        relay[j].wait_recv()
        over[3].append(go(share(at.far, j, 6, at.partner)))
        for kind in range(4):
            over[kind][j].wait_recv()
        product = dot(right[:, j].reshape(-1, tile), known[j])
        coeff[:, pl.ds(j * rank, rank)] = product.astype(BF16).reshape(local_rows, rank, sides_count)

    def multiply(g):
        first = GROUPS[g][0]

        def one(i, carry):
            term = dot(left[i + first].reshape(priors * rank, tile), coeff[i + first], TN)
            term = term.astype(BF16).reshape(at.nz, NX, thin, sides_count)
            for at_x in range(NX):
                prior[g].parts[at_x, :, i] = term[:, at_x]
            return carry

        lax.fori_loop(0, len(GROUPS[g]), one, 0)

    def own_base(g):
        total = prior[g].result()
        for i, a in enumerate(GROUPS[g]):
            updated[a] = sides[a] - total[i]

    multiply(0)
    prior[0].first()

    @pl.when(below)
    def _():
        lead_all.wait()
        product = dot(inverse[r % steps], lead_left[...].reshape(tile, half))
        lane = lax.broadcasted_iota(jnp.int32, product.shape, 1)
        packs[r, :, :half] = jnp.where(lane < r * rank, product, 0.0).astype(BF16)
        for copy in pack_copies:
            copy.start()

    multiply(1)
    multiply(2)
    prior[0].second()
    prior[1].first()
    for k in range(1, steps):

        @pl.when(r != k)
        def _():
            remote(packs.at[k], packs.at[k], pack_send.at[1], pack_recv.at[k], at.next_r[1], c).wait_recv()

    cross.source[0] = jnp.zeros(cross.source.shape[1:], BF16)
    for k in range(1, steps):
        lanes = lanes_of(k)
        wide[:, lanes] = packs[k, :, : lanes.stop - lanes.start]
        cross.source[k] = packs[k, :, :half]
        for m in range(steps):
            first = (local_rows + k - 1) * rank
            factors[m, :, first : first + rank] = packs[k, :, half + m * rank : half + (m + 1) * rank]
    cross.feed()
    factor_copies = at.start(factor_copies)
    own_factors[at.x] = factors[at.x]
    own_base(0)

    @pl.when(solving)
    def _():
        base_block[at.x] = updated[0].astype(BF16)
        running["base"] = at.start(base_copies, solving)

    multiply(3)

    @pl.when(solving)
    def _():
        landed(running["columns"])
        landed(running["base"])
        product = dot(columns[...].reshape(-1, LANES), base_block[...].reshape(-1, sides_count))
        start_parts[...] = product.astype(BF16).reshape(start_parts.shape)
        running["start"] = at.start(start_z_copies, solving)

    prior[1].second()
    prior[2].first()
    landed(factor_copies)
    cross.right(own_factors, local_rows, rank)

    @pl.when(solving)
    def _():
        landed(running["start"])
        total = start_parts[at.z].astype(F32)
        for d in range(1, at.nz):
            total = total + start_from[d].astype(F32)
        start[r % steps] = total.astype(BF16)
        for copy in start_copies:
            copy.start()

    prior[1].third()
    off = jnp.logical_and(at.z == 0, r <= at.x)
    for k in range(steps):

        @pl.when(r != k)
        def _():
            remote(start.at[k], start.at[k], start_send.at[1], start_recv.at[k], at.next_r[1], c).wait_recv()

    near.feed()
    prior[2].second()
    prior[3].first()
    near.right(own_factors, local_rows, rank)
    cross.share(rank, off)
    landed(left_copies)
    prior[2].third()
    cross.left(own_left)
    near.share(rank, off)
    prior[3].second()
    cross.lead_x()
    near.left(own_left)
    prior[3].third()
    near.lead_x()
    own_base(1)
    own_base(2)
    landed(cross.lead_copies)
    landed(cross.out_copies)
    landed(near.lead_copies)

    lead_coeff[...] = jnp.zeros(lead_coeff.shape, BF16)
    for m in range(steps - 1):
        for k in range(m + 1, steps):
            value = near.lead_rows(k, m)
            if m:
                lanes = lanes_of(m)
                size = lanes.stop - lanes.start
                value = value - dot(cross.lead_rows(k, m).astype(BF16)[:, :size], lead_coeff[lanes])
            first = lanes_of(k).start + m * rank
            lead_coeff[first : first + rank] = value.astype(BF16)
    for m in range(steps):
        answer = start[m].astype(F32)
        if m:
            answer = answer - dot(wide[:, lanes_of(m)], lead_coeff[lanes_of(m)])
        solved[m] = answer.astype(BF16)
    correction = dot(cross.whole[...].reshape(local_rows * thin, -1), lead_coeff[...])
    correction = correction.reshape(local_rows, thin, sides_count)
    own_base(3)
    landed(near.out_copies)
    for a in range(local_rows):
        updated[a] = updated[a] + (correction[a] - near.whole[a].astype(F32))

    for copy in at.sends:
        copy.close()

    @pl.when(below)
    def _():
        for copy in pack_copies:
            copy.wait_send()

    @pl.when(solving)
    def _():
        for copy in start_copies:
            copy.wait_send()


def place_results(updated, solved, updated_out, solved_out):
    for a in range(updated.shape[0]):
        updated_out[:, a] = updated[a]
    solved_out[...] = solved[...]


def local(right_sides, prior_left, prior_right, solved_prior, diag_left, diag_right, diag_inverse):
    thin, local_rows, sides = right_sides.shape
    priors, rank, tile = prior_left.shape[1:]
    diag_left, diag_right = jnp.swapaxes(diag_left, 2, 3), jnp.swapaxes(diag_right, 2, 3)
    steps = diag_left.shape[1]
    rows, cols = lax.axis_size(ROW), lax.axis_size(COL)
    nz = cols // NX
    width = steps * rank
    block = rank + CHUNK
    factor_width = (local_rows + NX - 1) * rank

    shapes = [
        prior_left.shape,
        prior_right.shape,
        (priors, tile, sides),
        (local_rows, priors * rank, sides),
        right_sides.shape,
        ((local_rows, thin, sides), F32),
        diag_left.shape,
        diag_right.shape,
        (local_rows, thin, width),
        diag_inverse.shape,
        (rows, thin, 4 * LANES),
        (nz, NX, thin, 2 * LANES),
        (steps, thin, factor_width),
        (NX, thin, factor_width),
        (nz, thin, width),
        (NX, thin, sides),
        (nz, thin, LANES),
        (nz, thin, sides),
        (nz, thin, sides),
        (thin, 4 * LANES),
        (4 * LANES, sides),
    ]
    one = (len(GROUPS[0]), thin, sides)
    shapes += [(NX, nz, *one), (NX - 1, nz, *one), (nz, *one), (nz, *one)]
    for group in GROUPS[1:]:
        for lead in ((NX, nz), (nz // 2,), (nz // 2,), (nz,), (nz,), (nz,), (nz,)):
            shapes.append((*lead, len(group), thin, sides))
    for out in (4 * LANES, sides):
        shapes += [
            (steps, thin, sides),
            (NX, thin, sides),
            (nz, block, sides),
            (nz, block, sides),
            (NX, rank, sides),
            (NX, nz, CHUNK, sides),
            (nz, thin, out),
            (nz, thin, out),
        ]
    scratch = [pltpu.VMEM(*shape) if isinstance(shape[0], tuple) else pltpu.VMEM(shape, BF16) for shape in shapes]
    bulk = len(GROUPS) - 1
    for shape in (
        (7,),
        (7, priors),
        (7, priors),
        (bulk, 6),
        (bulk, 6),
        (10, NX),
        (10, NX),
        (14, nz),
        (14, nz),
        (rows,),
        (steps,),
        (rows,),
        (steps,),
    ):
        scratch.append(pltpu.SemaphoreType.DMA(shape))
    updated, solved = pl.pallas_call(
        kernel,
        out_shape=(
            jax.ShapeDtypeStruct((local_rows, thin, sides), F32),
            jax.ShapeDtypeStruct((steps, thin, sides), BF16),
        ),
        in_specs=[pl.BlockSpec(memory_space=pl.ANY)] * 7,
        out_specs=(pl.BlockSpec(memory_space=pltpu.VMEM), pl.BlockSpec(memory_space=pltpu.VMEM)),
        scratch_shapes=scratch,
        compiler_params=pltpu.CompilerParams(
            collective_id=0, has_side_effects=True, vmem_limit_bytes=56 * 1024 * 1024
        ),
    )(right_sides, prior_left, prior_right, solved_prior, diag_left, diag_right, diag_inverse)
    return pl.pallas_call(
        place_results,
        out_shape=(
            jax.ShapeDtypeStruct((thin, local_rows, sides), F32),
            jax.ShapeDtypeStruct(solved.shape, BF16),
        ),
    )(updated, solved)


def solution(mesh):
    return jax.shard_map(
        local,
        mesh=mesh,
        in_specs=(
            P(COL, ROW, None),
            P(ROW, COL, None, None),
            P(ROW, COL, None, None),
            P(COL, ROW, None),
            P(ROW, None, None, COL),
            P(ROW, None, None, COL),
            P(None, COL, None),
        ),
        out_specs=(P(COL, ROW, None), P(None, COL, None)),
        check_vma=False,
    )
```

```python
import jax
import jax.numpy as jnp
from jax import lax
from jax.experimental import pallas as pl
from jax.experimental.pallas import tpu as pltpu
from jax.sharding import PartitionSpec as P

ROW = "row"
COL = "col"
CORES = 2
NX = 4
MESH = pl.DeviceIdType.MESH
F32 = jnp.float32
BF16 = jnp.bfloat16
LANES = 128
GROUPS = ((0,), (1, 2), (3, 4), (5, 6, 7))
CHUNK = 24
LEAD_X_AT = 3
TN = (((0,), (0,)), ((), ()))


def dot(a, b, dims=None):
    if dims is None:
        return jnp.dot(a, b, preferred_element_type=F32)
    return lax.dot_general(a, b, dims, preferred_element_type=F32)


def remote(src, dst, send, recv, row, col):
    return pltpu.make_async_remote_copy(
        src_ref=src,
        dst_ref=dst,
        send_sem=send,
        recv_sem=recv,
        device_id={ROW: row, COL: col},
        device_id_type=MESH,
    )


class Copy:
    def __init__(self, copy, only=None):
        self.copy, self.only, self.landed = copy, only, False

    def wait_recv(self):
        self.copy.wait_recv()
        self.landed = True

    def close(self):
        def rest():
            if not self.landed:
                self.copy.wait_recv()
            self.copy.wait_send()

        if self.only is None:
            rest()
        else:
            pl.when(self.only)(rest)


class Place:
    def __init__(self):
        self.rows, self.cols = lax.axis_size(ROW), lax.axis_size(COL)
        self.ny, self.nz = self.rows // CORES, self.cols // NX
        self.r, self.c = lax.axis_index(ROW), lax.axis_index(COL)
        self.y, self.q = self.r // CORES, self.r % CORES
        self.z, self.x = self.c // NX, self.c % NX
        self.up, self.down, self.far = (((self.y + d) % self.ny) * CORES + self.q for d in (1, self.ny - 1, 2))
        self.partner = self.y * CORES + 1 - self.q
        self.next_x = [(self.x + d) % NX for d in range(NX)]
        self.along_x = [self.z * NX + to for to in self.next_x]
        self.low, self.high = pl.ds(0, self.nz // 2), pl.ds(self.nz // 2, self.nz // 2)
        self.next_z = [(self.z + d) % self.nz for d in range(self.nz)]
        self.along_z = [to * NX + self.x for to in self.next_z]
        self.next_r = [(self.r + d) % self.rows for d in range(self.rows)]
        self.sends = []

    def go(self, copy, only=None):
        copy.start()
        tracked = Copy(copy, only)
        self.sends.append(tracked)
        return tracked

    def start(self, copies, only=None):
        return [self.go(copy, only) for copy in copies]

    def to_all_x(self, src, dst, sems):
        send, recv = sems
        return [
            remote(src(self.next_x[d]), dst(d), send.at[d], recv.at[d], self.r, self.along_x[d]) for d in (1, 3, 2)
        ]

    def to_all_z(self, src, dst, sems):
        send, recv = sems
        order = [4, 3, 5, 2, 6, 1, 7] if self.nz == 8 else range(1, self.nz)
        return [
            remote(src(self.next_z[d]), dst(d), send.at[d], recv.at[d], self.r, self.along_z[d]) for d in order
        ]


def landed(copies):
    for copy in copies:
        copy.wait_recv()


class Reduce:
    def __init__(self, at, buffers, x_sems, z_sems):
        self.at = at
        self.parts, self.from_a, self.from_b, self.from_l, self.from_r, self.part_sum, self.from_z = buffers
        self.x_send, self.x_recv = x_sems
        self.z_sems = z_sems
        self.copies = {}

    def send_x(self, kind, src, dst, d):
        at = self.at
        copy = remote(src, dst, self.x_send.at[kind], self.x_recv.at[kind], at.r, at.along_x[d])
        self.copies[kind] = at.go(copy)

    def first(self):
        at = self.at
        left, right, far = at.next_x[3], at.next_x[1], at.next_x[2]
        self.send_x(0, self.parts.at[far, at.low], self.from_a, 1)
        self.send_x(1, self.parts.at[far, at.high], self.from_b, 3)
        self.send_x(2, self.parts.at[right, at.high], self.from_l.at[at.high], 1)
        self.send_x(3, self.parts.at[left, at.low], self.from_r.at[at.low], 3)

    def second(self):
        at = self.at
        left, right = at.next_x[3], at.next_x[1]
        self.copies[0].wait_recv()
        own = self.parts[right, at.low].astype(F32)
        self.parts[right, at.low] = (own + self.from_a[...].astype(F32)).astype(BF16)
        self.send_x(4, self.parts.at[right, at.low], self.from_l.at[at.low], 1)
        self.copies[1].wait_recv()
        own = self.parts[left, at.high].astype(F32)
        self.parts[left, at.high] = (own + self.from_b[...].astype(F32)).astype(BF16)
        self.send_x(5, self.parts.at[left, at.high], self.from_r.at[at.high], 3)

    def third(self):
        at = self.at
        for kind in range(2, 6):
            self.copies[kind].wait_recv()

        def one(i, carry):
            total = self.parts[at.x, i].astype(F32) + self.from_l[i].astype(F32) + self.from_r[i].astype(F32)
            self.part_sum[i] = total.astype(BF16)
            return carry

        lax.fori_loop(0, at.nz, one, 0)
        self.send_z()

    def send_z(self):
        at = self.at
        self.z_copies = at.start(
            at.to_all_z(lambda to: self.part_sum.at[to], lambda d: self.from_z.at[d], self.z_sems)
        )

    def result(self):
        at = self.at
        landed(self.z_copies)
        total = self.part_sum[at.z].astype(F32)
        for d in range(1, at.nz):
            total = total + self.from_z[d].astype(F32)
        return total


class ReduceDirect(Reduce):
    def __init__(self, at, buffers, x_sems, z_sems):
        self.at = at
        self.parts, self.from_x, self.part_sum, self.from_z = buffers
        self.x_sems, self.z_sems = x_sems, z_sems

    def first(self):
        at = self.at
        self.x_copies = at.start(
            at.to_all_x(lambda to: self.parts.at[to], lambda d: self.from_x.at[d - 1], self.x_sems)
        )

    def second(self):
        at = self.at
        landed(self.x_copies)

        def one(i, carry):
            total = self.parts[at.x, i].astype(F32)
            for d in range(NX - 1):
                total = total + self.from_x[d, i].astype(F32)
            self.part_sum[i] = total.astype(BF16)
            return carry

        lax.fori_loop(0, at.nz, one, 0)
        self.send_z()


class Gather:
    def __init__(self, at, whole, x_sems, z_sems, only=None):
        self.at, self.whole, self.only = at, whole, only
        self.z_made = at.to_all_z(lambda to: whole.at[at.z, at.x], lambda d: whole.at[at.z, at.x], z_sems)
        self.x_made = at.to_all_x(lambda to: whole.at[:, at.x], lambda d: whole.at[:, at.x], x_sems)

    def first(self):
        self.z_copies = self.at.start(self.z_made, self.only)

    def second(self):
        landed(self.z_copies)
        self.x_copies = self.at.start(self.x_made, self.only)

    def wait(self):
        landed(self.x_copies)


class Flow:
    def __init__(self, at, buffers, sems, separate):
        self.at, self.separate = at, separate
        self.source, self.block, self.parts, self.from_z, self.steps, self.lead, self.out, self.whole = buffers[:8]
        self.lead_parts, self.lead_from_z = buffers[8:]
        self.sems = sems

    def feed(self):
        at = self.at
        self.block[at.x] = self.source[at.x]
        self.fed = at.start(
            at.to_all_x(lambda to: self.source.at[to], lambda d: self.block.at[at.x], self.sems[0])
        )

    def right(self, factors, positions, rank):
        at = self.at
        landed(self.fed)
        count, thin, sides = self.block.shape
        product = dot(factors[...].reshape(count * thin, -1), self.block[...].reshape(count * thin, sides), TN)
        self.parts[...] = product[: positions * rank].astype(BF16).reshape(positions, rank, sides)
        self.z_copies = at.start(
            at.to_all_z(lambda to: self.parts.at[to], lambda d: self.from_z.at[d], self.sems[1])
        )
        lead = product[positions * rank :]
        chunks = (NX - 1) * rank // CHUNK
        for i in range(at.nz):
            part = lead[i * CHUNK : (i + 1) * CHUNK] if i < chunks else jnp.zeros((CHUNK, sides), F32)
            self.lead_parts[i] = part.astype(BF16)
        self.lead_sums = at.start(
            at.to_all_z(lambda to: self.lead_parts.at[to], lambda d: self.lead_from_z.at[d], self.sems[6])
        )

    def share(self, off):
        at = self.at
        landed(self.z_copies)
        total = self.parts[at.z].astype(F32)
        for d in range(1, at.nz):
            total = total + self.from_z[d].astype(F32)
        self.steps[at.x] = jnp.where(off, 0.0, total).astype(BF16)
        self.x_copies = at.start(
            at.to_all_x(lambda to: self.steps.at[at.x], lambda d: self.steps.at[at.x], self.sems[2])
        )

    def lead_z(self):
        at = self.at
        landed(self.lead_sums)
        total = self.lead_parts[at.z].astype(F32)
        for d in range(1, at.nz):
            total = total + self.lead_from_z[d].astype(F32)
        self.lead[at.x, at.z] = total.astype(BF16)
        own = self.lead.at[at.x, at.z]
        self.lead_all = at.start(at.to_all_z(lambda to: own, lambda d: own, self.sems[3]))

    def left(self, factors):
        at = self.at
        landed(self.x_copies)
        nz, thin, width = factors.shape
        rows = factors[...].reshape(nz * thin, width)
        rank = self.steps.shape[1]
        if self.separate:
            for m in range(1, NX):
                lanes = lanes_of(m)
                product = dot(rows[:, m * rank : (m + 1) * rank], self.steps[m, :, : lanes.stop - lanes.start])
                self.out[:, :, lanes] = product.astype(BF16).reshape(nz, thin, -1)
        else:
            product = dot(rows, self.steps[...].reshape(width, -1))
            self.out[...] = product.astype(BF16).reshape(nz, thin, -1)
        self.whole[at.z] = self.out[at.z]
        self.out_copies = at.start(
            at.to_all_z(lambda to: self.out.at[to], lambda d: self.whole.at[at.z], self.sems[4])
        )

    def lead_x(self):
        at = self.at
        landed(self.lead_all)
        own = self.lead.at[at.x]
        self.lead_copies = at.start(at.to_all_x(lambda to: own, lambda d: own, self.sems[5]))

    def lead_rows(self, k, m):
        rank = self.steps.shape[1]
        pieces = rank // CHUNK
        first = (k - 1) * pieces
        return jnp.concatenate([self.lead[m, first + i].astype(F32) for i in range(pieces)], axis=0)


def lanes_of(m):
    first = (None, 0, LANES, 2 * LANES)[m]
    return slice(first, first + (LANES if m < 3 else 2 * LANES))


def take(refs, count):
    return [refs.pop(0) for _ in range(count)]


def kernel(sides_in, left_in, right_in, known_in, dleft_in, dright_in, inverse_in, updated, solved, *scratch):
    at = Place()
    r, c, go = at.r, at.c, at.go
    refs = list(scratch)
    left, right, known, coeff, sides_raw, sides, dleft_raw, dright_raw, dleft, inverse = take(refs, 10)
    packs, lead_left, factors, own_factors, own_left = take(refs, 5)
    base_block, columns, start_parts, start_from = take(refs, 4)
    wide, lead_coeff = take(refs, 2)
    lead_buffers = take(refs, 4)
    bulk_buffers = [take(refs, 7) for _ in GROUPS[1:]]
    flow_buffers = [take(refs, 10) for _ in range(2)]
    start = flow_buffers[1][0]
    load_sem, gather_send, gather_recv, bulk_send, bulk_recv = take(refs, 5)
    x_send, x_recv, z_send, z_recv = take(refs, 4)
    pack_send, pack_recv, start_send, start_recv = take(refs, 4)
    x_sems = [(x_send.at[i], x_recv.at[i]) for i in range(x_send.shape[0])]
    z_sems = [(z_send.at[i], z_recv.at[i]) for i in range(z_send.shape[0])]

    depth, priors = known_in.shape[1], known_in.shape[0]
    local_rows, steps, thin, rank = dleft_in.shape
    sides_count = sides.shape[2]
    tile = left.shape[3]
    width = steps * rank
    half = packs.shape[2] // 2
    solving = r < steps
    below = jnp.logical_and(r > 0, solving)

    prior = [ReduceDirect(at, lead_buffers, x_sems.pop(), z_sems.pop())]
    for i, buffers in enumerate(bulk_buffers):
        prior.append(Reduce(at, buffers, (bulk_send.at[i], bulk_recv.at[i]), z_sems.pop()))
    lead_all = Gather(at, lead_left, x_sems.pop(), z_sems.pop(), below)
    base_copies = at.to_all_x(lambda to: base_block.at[at.x], lambda d: base_block.at[at.x], x_sems.pop())
    start_z_copies = at.to_all_z(lambda to: start_parts.at[to], lambda d: start_from.at[d], z_sems.pop())
    column_copies = at.to_all_z(
        lambda to: inverse.at[r % steps, :, pl.ds(pl.multiple_of(to * LANES, LANES), LANES)],
        lambda d: columns.at[at.z],
        z_sems.pop(),
    )
    start_copies = [
        remote(start.at[r % steps], start.at[r % steps], start_send.at[d], start_recv.at[r % steps], at.next_r[d], c)
        for d in range(1, at.rows)
    ]
    pack_copies = [
        remote(packs.at[r], packs.at[r], pack_send.at[d], pack_recv.at[r % steps], at.next_r[d], c)
        for d in range(1, at.rows)
    ]
    running = {}
    flows = [
        Flow(
            at,
            buffers,
            (x_sems.pop(), z_sems.pop(), x_sems.pop(), z_sems.pop(), z_sems.pop(), x_sems.pop(), z_sems.pop()),
            separate,
        )
        for buffers, separate in zip(flow_buffers, (True, False))
    ]
    cross, near = flows
    factor_copies = at.to_all_x(lambda to: factors.at[to], lambda d: own_factors.at[at.x], x_sems.pop())
    left_copies = at.to_all_z(lambda to: dleft.at[to], lambda d: own_left.at[at.z], z_sems.pop())

    loads = [
        pltpu.make_async_copy(src, dst, load_sem.at[i])
        for i, (src, dst) in enumerate(
            (
                (known_in, known.at[:, pl.ds(r * depth, depth)]),
                (dleft_in, dleft_raw),
                (dright_in, dright_raw),
                (inverse_in, inverse),
                (right_in, right),
                (left_in, left),
                (sides_in, sides_raw),
            )
        )
    ]
    for load in loads:
        load.start()
    barrier = pltpu.get_barrier_semaphore()
    peers = [(at.next_r[d], c) for d in range(1, at.rows)]
    peers += [(r, at.along_x[d]) for d in range(1, NX)]
    peers += [(r, at.along_z[d]) for d in range(1, at.nz)]
    for row, col in peers:
        pl.semaphore_signal(barrier, inc=1, device_id={ROW: row, COL: col}, device_id_type=MESH)

    loads[0].wait()
    pl.semaphore_wait(barrier, len(peers))

    def block(row, j):
        return known.at[j, pl.ds(row * depth, depth)]

    def share(row_of_block, j, kind, target):
        part = block(row_of_block, j)
        return remote(part, part, gather_send.at[kind, j], gather_recv.at[kind, j], target, c)

    own_up, own_down, relay, over = [], [], [], [[], [], [], []]
    for j in range(priors):
        own_up.append(go(share(r, j, 0, at.up)))
        own_down.append(go(share(r, j, 1, at.down)))
        over[0].append(go(share(r, j, 3, at.partner)))
    for load in loads[1:3]:
        load.wait()
    factors[...] = jnp.zeros(factors.shape, BF16)
    packs[r] = jnp.zeros(packs.shape[1:], BF16)
    for m in range(steps):
        lanes = slice(m * rank, (m + 1) * rank)
        packs[r, :, half + m * rank : half + (m + 1) * rank] = dright_raw[0, m]
        for a in range(local_rows):
            dleft[a, :, lanes] = dleft_raw[a, m]
            factors[m, :, a * rank : (a + 1) * rank] = dright_raw[a, m]
    lead_left[at.z, at.x] = jnp.zeros(lead_left.shape[2:], BF16)
    for m in range(steps - 1):
        lead_left[at.z, at.x, :, m * rank : (m + 1) * rank] = dleft_raw[0, m]

    @pl.when(below)
    def _():
        lead_all.first()

    loads[3].wait()

    @pl.when(solving)
    def _():
        running["columns"] = at.start(column_copies, solving)
        columns[at.z] = inverse[r % steps, :, pl.ds(pl.multiple_of(at.z * LANES, LANES), LANES)]

    left_copies = at.start(left_copies)
    own_left[at.z] = dleft[at.z]
    for j in range(priors):
        own_up[j].wait_recv()
        over[1].append(go(share(at.down, j, 4, at.partner)))
        if j < priors // 2:
            relay.append(go(share(at.down, j, 2, at.up)))
        own_down[j].wait_recv()
        over[2].append(go(share(at.up, j, 5, at.partner)))
        if j >= priors // 2:
            relay.append(go(share(at.up, j, 2, at.down)))
        if j == LEAD_X_AT:

            @pl.when(below)
            def _():
                lead_all.second()

    loads[6].wait()
    whole_sides = sides_raw[...].astype(F32)
    for a in range(local_rows):
        sides[a] = whole_sides[:, a]

    for load in loads[4:6]:
        load.wait()
    for j in range(priors):
        relay[j].wait_recv()
        over[3].append(go(share(at.far, j, 6, at.partner)))
        for kind in range(4):
            over[kind][j].wait_recv()
        product = dot(right[:, j].reshape(-1, tile), known[j])
        coeff[:, pl.ds(j * rank, rank)] = product.astype(BF16).reshape(local_rows, rank, sides_count)

    def multiply(g):
        first = GROUPS[g][0]

        def one(i, carry):
            term = dot(left[i + first].reshape(priors * rank, tile), coeff[i + first], TN)
            term = term.astype(BF16).reshape(at.nz, NX, thin, sides_count)
            for at_x in range(NX):
                prior[g].parts[at_x, :, i] = term[:, at_x]
            return carry

        lax.fori_loop(0, len(GROUPS[g]), one, 0)

    def own_base(g):
        total = prior[g].result()
        for i, a in enumerate(GROUPS[g]):
            updated[a] = sides[a] - total[i]

    multiply(0)
    prior[0].first()
    @pl.when(below)
    def _():
        lead_all.wait()
        product = dot(inverse[r % steps], lead_left[...].reshape(tile, half))
        lane = lax.broadcasted_iota(jnp.int32, product.shape, 1)
        packs[r, :, :half] = jnp.where(lane < r * rank, product, 0.0).astype(BF16)
        for copy in pack_copies:
            copy.start()

    multiply(1)
    multiply(2)
    prior[0].second()
    for k in range(1, steps):

        @pl.when(r != k)
        def _():
            remote(packs.at[k], packs.at[k], pack_send.at[1], pack_recv.at[k], at.next_r[1], c).wait_recv()

    cross.source[0] = jnp.zeros(cross.source.shape[1:], BF16)
    for k in range(1, steps):
        lanes = lanes_of(k)
        wide[:, lanes] = packs[k, :, : lanes.stop - lanes.start]
        cross.source[k] = packs[k, :, :half]
        for m in range(steps):
            first = (local_rows + k - 1) * rank
            factors[m, :, first : first + rank] = packs[k, :, half + m * rank : half + (m + 1) * rank]
    cross.feed()
    factor_copies = at.start(factor_copies)
    own_factors[at.x] = factors[at.x]
    prior[1].first()
    own_base(0)
    @pl.when(solving)
    def _():
        base_block[at.x] = updated[0].astype(BF16)
        running["base"] = at.start(base_copies, solving)

    landed(factor_copies)
    cross.right(own_factors, local_rows, rank)
    multiply(3)
    @pl.when(solving)
    def _():
        landed(running["columns"])
        landed(running["base"])
        product = dot(columns[...].reshape(-1, LANES), base_block[...].reshape(-1, sides_count))
        start_parts[...] = product.astype(BF16).reshape(start_parts.shape)
        running["start"] = at.start(start_z_copies, solving)

    prior[1].second()
    prior[2].first()
    off = jnp.logical_and(at.z == 0, r <= at.x)
    @pl.when(solving)
    def _():
        landed(running["start"])
        total = start_parts[at.z].astype(F32)
        for d in range(1, at.nz):
            total = total + start_from[d].astype(F32)
        start[r % steps] = total.astype(BF16)
        for copy in start_copies:
            copy.start()

    prior[1].third()
    cross.share(off)
    cross.lead_z()
    for k in range(steps):

        @pl.when(r != k)
        def _():
            remote(start.at[k], start.at[k], start_send.at[1], start_recv.at[k], at.next_r[1], c).wait_recv()

    near.feed()
    prior[2].second()
    prior[3].first()
    near.right(own_factors, local_rows, rank)
    landed(left_copies)
    cross.left(own_left)
    cross.lead_x()
    prior[2].third()
    near.share(off)
    near.lead_z()
    prior[3].second()
    near.left(own_left)
    prior[3].third()
    near.lead_x()
    own_base(1)
    own_base(2)
    landed(cross.lead_copies)
    landed(cross.out_copies)
    landed(near.lead_copies)

    lead_coeff[...] = jnp.zeros(lead_coeff.shape, BF16)
    for m in range(steps - 1):
        for k in range(m + 1, steps):
            value = near.lead_rows(k, m)
            if m:
                lanes = lanes_of(m)
                size = lanes.stop - lanes.start
                value = value - dot(cross.lead_rows(k, m).astype(BF16)[:, :size], lead_coeff[lanes])
            first = lanes_of(k).start + m * rank
            lead_coeff[first : first + rank] = value.astype(BF16)
    for m in range(steps):
        answer = start[m].astype(F32)
        if m:
            answer = answer - dot(wide[:, lanes_of(m)], lead_coeff[lanes_of(m)])
        solved[m] = answer.astype(BF16)
    correction = dot(cross.whole[...].reshape(local_rows * thin, -1), lead_coeff[...])
    correction = correction.reshape(local_rows, thin, sides_count)
    own_base(3)
    landed(near.out_copies)
    for a in range(local_rows):
        updated[a] = updated[a] + (correction[a] - near.whole[a].astype(F32))

    for copy in at.sends:
        copy.close()

    @pl.when(below)
    def _():
        for copy in pack_copies:
            copy.wait_send()

    @pl.when(solving)
    def _():
        for copy in start_copies:
            copy.wait_send()


def place_results(updated, solved, updated_out, solved_out):
    for a in range(updated.shape[0]):
        updated_out[:, a] = updated[a]
    solved_out[...] = solved[...]


def local(right_sides, prior_left, prior_right, solved_prior, diag_left, diag_right, diag_inverse):
    thin, local_rows, sides = right_sides.shape
    priors, rank, tile = prior_left.shape[1:]
    diag_left, diag_right = jnp.swapaxes(diag_left, 2, 3), jnp.swapaxes(diag_right, 2, 3)
    steps = diag_left.shape[1]
    rows, cols = lax.axis_size(ROW), lax.axis_size(COL)
    nz = cols // NX
    width = steps * rank
    factor_width = (local_rows + NX - 1) * rank

    shapes = [
        prior_left.shape,
        prior_right.shape,
        (priors, tile, sides),
        (local_rows, priors * rank, sides),
        right_sides.shape,
        ((local_rows, thin, sides), F32),
        diag_left.shape,
        diag_right.shape,
        (local_rows, thin, width),
        diag_inverse.shape,
        (rows, thin, 4 * LANES),
        (nz, NX, thin, 2 * LANES),
        (steps, thin, factor_width),
        (NX, thin, factor_width),
        (nz, thin, width),
        (NX, thin, sides),
        (nz, thin, LANES),
        (nz, thin, sides),
        (nz, thin, sides),
        (thin, 4 * LANES),
        (4 * LANES, sides),
    ]
    one = (len(GROUPS[0]), thin, sides)
    shapes += [(NX, nz, *one), (NX - 1, nz, *one), (nz, *one), (nz, *one)]
    for group in GROUPS[1:]:
        for lead in ((NX, nz), (nz // 2,), (nz // 2,), (nz,), (nz,), (nz,), (nz,)):
            shapes.append((*lead, len(group), thin, sides))
    for out in (4 * LANES, sides):
        shapes += [
            (steps, thin, sides),
            (NX, thin, sides),
            (nz, rank, sides),
            (nz, rank, sides),
            (NX, rank, sides),
            (NX, nz, CHUNK, sides),
            (nz, thin, out),
            (nz, thin, out),
            (nz, CHUNK, sides),
            (nz, CHUNK, sides),
        ]
    scratch = [pltpu.VMEM(*shape) if isinstance(shape[0], tuple) else pltpu.VMEM(shape, BF16) for shape in shapes]
    bulk = len(GROUPS) - 1
    for shape in (
        (7,),
        (7, priors),
        (7, priors),
        (bulk, 6),
        (bulk, 6),
        (10, NX),
        (10, NX),
        (17, nz),
        (17, nz),
        (rows,),
        (steps,),
        (rows,),
        (steps,),
    ):
        scratch.append(pltpu.SemaphoreType.DMA(shape))
    updated, solved = pl.pallas_call(
        kernel,
        out_shape=(
            jax.ShapeDtypeStruct((local_rows, thin, sides), F32),
            jax.ShapeDtypeStruct((steps, thin, sides), BF16),
        ),
        in_specs=[pl.BlockSpec(memory_space=pl.ANY)] * 7,
        out_specs=(pl.BlockSpec(memory_space=pltpu.VMEM), pl.BlockSpec(memory_space=pltpu.VMEM)),
        scratch_shapes=scratch,
        compiler_params=pltpu.CompilerParams(
            collective_id=0, has_side_effects=True, vmem_limit_bytes=56 * 1024 * 1024
        ),
    )(right_sides, prior_left, prior_right, solved_prior, diag_left, diag_right, diag_inverse)
    return pl.pallas_call(
        place_results,
        out_shape=(
            jax.ShapeDtypeStruct((thin, local_rows, sides), F32),
            jax.ShapeDtypeStruct(solved.shape, BF16),
        ),
    )(updated, solved)


def solution(mesh):
    return jax.shard_map(
        local,
        mesh=mesh,
        in_specs=(
            P(COL, ROW, None),
            P(ROW, COL, None, None),
            P(ROW, COL, None, None),
            P(COL, ROW, None),
            P(ROW, None, None, COL),
            P(ROW, None, None, COL),
            P(None, COL, None),
        ),
        out_specs=(P(COL, ROW, None), P(None, COL, None)),
        check_vma=False,
    )
```

```python
import jax
import jax.numpy as jnp
from jax import lax
from jax.experimental import pallas as pl
from jax.experimental.pallas import tpu as pltpu
from jax.sharding import PartitionSpec as P

ROW = "row"
COL = "col"
CORES = 2
NX = 4
MESH = pl.DeviceIdType.MESH
F32 = jnp.float32
BF16 = jnp.bfloat16
LANES = 128
GROUPS = ((0,), (1, 2), (3, 4), (5, 6, 7))
CHUNK = 24
LEAD_X_AT = 3
TN = (((0,), (0,)), ((), ()))


def dot(a, b, dims=None):
    if dims is None:
        return jnp.dot(a, b, preferred_element_type=F32)
    return lax.dot_general(a, b, dims, preferred_element_type=F32)


def remote(src, dst, send, recv, row, col):
    return pltpu.make_async_remote_copy(
        src_ref=src,
        dst_ref=dst,
        send_sem=send,
        recv_sem=recv,
        device_id={ROW: row, COL: col},
        device_id_type=MESH,
    )


class Copy:
    def __init__(self, copy, only=None):
        self.copy, self.only, self.landed = copy, only, False

    def wait_recv(self):
        self.copy.wait_recv()
        self.landed = True

    def close(self):
        def rest():
            if not self.landed:
                self.copy.wait_recv()
            self.copy.wait_send()

        if self.only is None:
            rest()
        else:
            pl.when(self.only)(rest)


class Place:
    def __init__(self):
        self.rows, self.cols = lax.axis_size(ROW), lax.axis_size(COL)
        self.ny, self.nz = self.rows // CORES, self.cols // NX
        self.r, self.c = lax.axis_index(ROW), lax.axis_index(COL)
        self.y, self.q = self.r // CORES, self.r % CORES
        self.z, self.x = self.c // NX, self.c % NX
        self.up, self.down, self.far = (((self.y + d) % self.ny) * CORES + self.q for d in (1, self.ny - 1, 2))
        self.partner = self.y * CORES + 1 - self.q
        self.next_x = [(self.x + d) % NX for d in range(NX)]
        self.along_x = [self.z * NX + to for to in self.next_x]
        self.low, self.high = pl.ds(0, self.nz // 2), pl.ds(self.nz // 2, self.nz // 2)
        self.next_z = [(self.z + d) % self.nz for d in range(self.nz)]
        self.along_z = [to * NX + self.x for to in self.next_z]
        self.next_r = [(self.r + d) % self.rows for d in range(self.rows)]
        self.sends = []

    def go(self, copy, only=None):
        copy.start()
        tracked = Copy(copy, only)
        self.sends.append(tracked)
        return tracked

    def start(self, copies, only=None):
        return [self.go(copy, only) for copy in copies]

    def to_all_x(self, src, dst, sems):
        send, recv = sems
        return [
            remote(src(self.next_x[d]), dst(d), send.at[d], recv.at[d], self.r, self.along_x[d]) for d in (1, 3, 2)
        ]

    def to_all_z(self, src, dst, sems):
        send, recv = sems
        order = [4, 3, 5, 2, 6, 1, 7] if self.nz == 8 else range(1, self.nz)
        return [
            remote(src(self.next_z[d]), dst(d), send.at[d], recv.at[d], self.r, self.along_z[d]) for d in order
        ]


def landed(copies):
    for copy in copies:
        copy.wait_recv()


class Reduce:
    def __init__(self, at, buffers, x_sems, z_sems):
        self.at = at
        self.parts, self.from_a, self.from_b, self.from_l, self.from_r, self.part_sum, self.from_z = buffers
        self.x_send, self.x_recv = x_sems
        self.z_sems = z_sems
        self.copies = {}

    def send_x(self, kind, src, dst, d):
        at = self.at
        copy = remote(src, dst, self.x_send.at[kind], self.x_recv.at[kind], at.r, at.along_x[d])
        self.copies[kind] = at.go(copy)

    def first(self):
        at = self.at
        left, right, far = at.next_x[3], at.next_x[1], at.next_x[2]
        self.send_x(0, self.parts.at[far, at.low], self.from_a, 1)
        self.send_x(1, self.parts.at[far, at.high], self.from_b, 3)
        self.send_x(2, self.parts.at[right, at.high], self.from_l.at[at.high], 1)
        self.send_x(3, self.parts.at[left, at.low], self.from_r.at[at.low], 3)

    def second(self):
        at = self.at
        left, right = at.next_x[3], at.next_x[1]
        self.copies[0].wait_recv()
        own = self.parts[right, at.low].astype(F32)
        self.parts[right, at.low] = (own + self.from_a[...].astype(F32)).astype(BF16)
        self.send_x(4, self.parts.at[right, at.low], self.from_l.at[at.low], 1)
        self.copies[1].wait_recv()
        own = self.parts[left, at.high].astype(F32)
        self.parts[left, at.high] = (own + self.from_b[...].astype(F32)).astype(BF16)
        self.send_x(5, self.parts.at[left, at.high], self.from_r.at[at.high], 3)

    def third(self):
        at = self.at
        for kind in range(2, 6):
            self.copies[kind].wait_recv()

        def one(i, carry):
            total = self.parts[at.x, i].astype(F32) + self.from_l[i].astype(F32) + self.from_r[i].astype(F32)
            self.part_sum[i] = total.astype(BF16)
            return carry

        lax.fori_loop(0, at.nz, one, 0)
        self.send_z()

    def send_z(self):
        at = self.at
        self.z_copies = at.start(
            at.to_all_z(lambda to: self.part_sum.at[to], lambda d: self.from_z.at[d], self.z_sems)
        )

    def result(self):
        at = self.at
        landed(self.z_copies)
        total = self.part_sum[at.z].astype(F32)
        for d in range(1, at.nz):
            total = total + self.from_z[d].astype(F32)
        return total


class ReduceDirect(Reduce):
    def __init__(self, at, buffers, x_sems, z_sems):
        self.at = at
        self.parts, self.from_x, self.part_sum, self.from_z = buffers
        self.x_sems, self.z_sems = x_sems, z_sems

    def first(self):
        at = self.at
        self.x_copies = at.start(
            at.to_all_x(lambda to: self.parts.at[to], lambda d: self.from_x.at[d - 1], self.x_sems)
        )

    def second(self):
        at = self.at
        landed(self.x_copies)

        def one(i, carry):
            total = self.parts[at.x, i].astype(F32)
            for d in range(NX - 1):
                total = total + self.from_x[d, i].astype(F32)
            self.part_sum[i] = total.astype(BF16)
            return carry

        lax.fori_loop(0, at.nz, one, 0)
        self.send_z()


class Gather:
    def __init__(self, at, whole, x_sems, z_sems, only=None):
        self.at, self.whole, self.only = at, whole, only
        self.z_made = at.to_all_z(lambda to: whole.at[at.z, at.x], lambda d: whole.at[at.z, at.x], z_sems)
        self.x_made = at.to_all_x(lambda to: whole.at[:, at.x], lambda d: whole.at[:, at.x], x_sems)

    def first(self):
        self.z_copies = self.at.start(self.z_made, self.only)

    def second(self):
        landed(self.z_copies)
        self.x_copies = self.at.start(self.x_made, self.only)

    def wait(self):
        landed(self.x_copies)


class Flow:
    def __init__(self, at, buffers, sems, separate):
        self.at, self.separate = at, separate
        self.source, self.block, self.parts, self.from_z, self.steps, self.lead, self.out, self.whole = buffers[:8]
        self.lead_parts, self.lead_from_z = buffers[8:]
        self.sems = sems

    def feed(self):
        at = self.at
        self.block[at.x] = self.source[at.x]
        self.fed = at.start(
            at.to_all_x(lambda to: self.source.at[to], lambda d: self.block.at[at.x], self.sems[0])
        )

    def right(self, factors, positions, rank):
        at = self.at
        landed(self.fed)
        count, thin, sides = self.block.shape
        product = dot(factors[...].reshape(count * thin, -1), self.block[...].reshape(count * thin, sides), TN)
        self.parts[...] = product[: positions * rank].astype(BF16).reshape(positions, rank, sides)
        self.z_copies = at.start(
            at.to_all_z(lambda to: self.parts.at[to], lambda d: self.from_z.at[d], self.sems[1])
        )
        lead = product[positions * rank :]
        chunks = (NX - 1) * rank // CHUNK
        for i in range(at.nz):
            part = lead[i * CHUNK : (i + 1) * CHUNK] if i < chunks else jnp.zeros((CHUNK, sides), F32)
            self.lead_parts[i] = part[:, : self.lead_parts.shape[2]].astype(BF16)
        self.lead_sums = at.start(
            at.to_all_z(lambda to: self.lead_parts.at[to], lambda d: self.lead_from_z.at[d], self.sems[6])
        )

    def share(self, off):
        at = self.at
        landed(self.z_copies)
        total = self.parts[at.z].astype(F32)
        for d in range(1, at.nz):
            total = total + self.from_z[d].astype(F32)
        self.steps[at.x] = jnp.where(off, 0.0, total).astype(BF16)
        self.x_copies = at.start(
            at.to_all_x(lambda to: self.steps.at[at.x], lambda d: self.steps.at[at.x], self.sems[2])
        )

    def lead_z(self):
        at = self.at
        landed(self.lead_sums)
        total = self.lead_parts[at.z].astype(F32)
        for d in range(1, at.nz):
            total = total + self.lead_from_z[d].astype(F32)
        self.lead[at.x, at.z] = total.astype(BF16)
        own = self.lead.at[at.x, at.z]
        self.lead_all = at.start(at.to_all_z(lambda to: own, lambda d: own, self.sems[3]))

    def left(self, factors):
        at = self.at
        landed(self.x_copies)
        nz, thin, width = factors.shape
        rows = factors[...].reshape(nz * thin, width)
        rank = self.steps.shape[1]
        if self.separate:
            for m in range(1, NX):
                lanes = lanes_of(m)
                product = dot(rows[:, m * rank : (m + 1) * rank], self.steps[m, :, : lanes.stop - lanes.start])
                first = m * (m - 1) // 2 * rank
                product = product[:, : m * rank].astype(BF16).reshape(nz, thin, m * rank)
                self.out[:, :, first : first + m * rank] = product
        else:
            product = dot(rows, self.steps[...].reshape(width, -1))
            self.out[...] = product.astype(BF16).reshape(nz, thin, -1)
        self.whole[at.z] = self.out[at.z]
        self.out_copies = at.start(
            at.to_all_z(lambda to: self.out.at[to], lambda d: self.whole.at[at.z], self.sems[4])
        )

    def lead_x(self):
        at = self.at
        landed(self.lead_all)
        own = self.lead.at[at.x, pl.ds(0, (NX - 1) * self.steps.shape[1] // CHUNK)]
        self.lead_copies = at.start(at.to_all_x(lambda to: own, lambda d: own, self.sems[5]))

    def lead_rows(self, k, m):
        rank = self.steps.shape[1]
        pieces = rank // CHUNK
        first = (k - 1) * pieces
        return jnp.concatenate([self.lead[m, first + i].astype(F32) for i in range(pieces)], axis=0)


def lanes_of(m):
    first = (None, 0, LANES, 2 * LANES)[m]
    return slice(first, first + (LANES if m < 3 else 2 * LANES))


def take(refs, count):
    return [refs.pop(0) for _ in range(count)]


def kernel(sides_in, left_in, right_in, known_in, dleft_in, dright_in, inverse_in, updated, solved, *scratch):
    at = Place()
    r, c, go = at.r, at.c, at.go
    refs = list(scratch)
    left, right, known, coeff, sides_raw, sides, dleft_raw, dright_raw, dleft, inverse = take(refs, 10)
    packs, lead_left, factors, own_factors, own_left = take(refs, 5)
    base_block, columns, start_parts, start_from = take(refs, 4)
    wide, lead_coeff, joined = take(refs, 3)
    lead_buffers = take(refs, 4)
    bulk_buffers = [take(refs, 7) for _ in GROUPS[1:]]
    flow_buffers = [take(refs, 10) for _ in range(2)]
    start = flow_buffers[1][0]
    load_sem, gather_send, gather_recv, bulk_send, bulk_recv = take(refs, 5)
    x_send, x_recv, z_send, z_recv = take(refs, 4)
    pack_send, pack_recv, start_send, start_recv = take(refs, 4)
    x_sems = [(x_send.at[i], x_recv.at[i]) for i in range(x_send.shape[0])]
    z_sems = [(z_send.at[i], z_recv.at[i]) for i in range(z_send.shape[0])]

    depth, priors = known_in.shape[1], known_in.shape[0]
    local_rows, steps, thin, rank = dleft_in.shape
    sides_count = sides.shape[2]
    tile = left.shape[3]
    width = steps * rank
    half = packs.shape[2] // 2
    solving = r < steps
    below = jnp.logical_and(r > 0, solving)

    prior = [ReduceDirect(at, lead_buffers, x_sems.pop(), z_sems.pop())]
    for i, buffers in enumerate(bulk_buffers):
        prior.append(Reduce(at, buffers, (bulk_send.at[i], bulk_recv.at[i]), z_sems.pop()))
    lead_all = Gather(at, lead_left, x_sems.pop(), z_sems.pop(), below)
    base_copies = at.to_all_x(lambda to: base_block.at[at.x], lambda d: base_block.at[at.x], x_sems.pop())
    start_z_copies = at.to_all_z(lambda to: start_parts.at[to], lambda d: start_from.at[d], z_sems.pop())
    column_copies = at.to_all_z(
        lambda to: inverse.at[r % steps, :, pl.ds(pl.multiple_of(to * LANES, LANES), LANES)],
        lambda d: columns.at[at.z],
        z_sems.pop(),
    )
    start_copies = [
        remote(start.at[r % steps], start.at[r % steps], start_send.at[d], start_recv.at[r % steps], at.next_r[d], c)
        for d in range(1, at.rows)
    ]
    pack_copies = [
        remote(packs.at[r], packs.at[r], pack_send.at[d], pack_recv.at[r % steps], at.next_r[d], c)
        for d in range(1, at.rows)
    ]
    running = {}
    flows = [
        Flow(
            at,
            buffers,
            (x_sems.pop(), z_sems.pop(), x_sems.pop(), z_sems.pop(), z_sems.pop(), x_sems.pop(), z_sems.pop()),
            separate,
        )
        for buffers, separate in zip(flow_buffers, (True, False))
    ]
    cross, near = flows
    factor_copies = at.to_all_x(lambda to: factors.at[to], lambda d: own_factors.at[at.x], x_sems.pop())
    left_copies = at.to_all_z(lambda to: dleft.at[to], lambda d: own_left.at[at.z], z_sems.pop())

    loads = [
        pltpu.make_async_copy(src, dst, load_sem.at[i])
        for i, (src, dst) in enumerate(
            (
                (known_in, known.at[:, pl.ds(r * depth, depth)]),
                (dleft_in, dleft_raw),
                (dright_in, dright_raw),
                (inverse_in, inverse),
                (right_in, right),
                (left_in, left),
                (sides_in, sides_raw),
            )
        )
    ]
    for load in loads:
        load.start()
    barrier = pltpu.get_barrier_semaphore()
    peers = [(at.next_r[d], c) for d in range(1, at.rows)]
    peers += [(r, at.along_x[d]) for d in range(1, NX)]
    peers += [(r, at.along_z[d]) for d in range(1, at.nz)]
    for row, col in peers:
        pl.semaphore_signal(barrier, inc=1, device_id={ROW: row, COL: col}, device_id_type=MESH)

    loads[0].wait()
    pl.semaphore_wait(barrier, len(peers))

    def block(row, j):
        return known.at[j, pl.ds(row * depth, depth)]

    def share(row_of_block, j, kind, target):
        part = block(row_of_block, j)
        return remote(part, part, gather_send.at[kind, j], gather_recv.at[kind, j], target, c)

    own_up, own_down, relay, over = [], [], [], [[], [], [], []]
    for j in range(priors):
        own_up.append(go(share(r, j, 0, at.up)))
        own_down.append(go(share(r, j, 1, at.down)))
        over[0].append(go(share(r, j, 3, at.partner)))
    for load in loads[1:3]:
        load.wait()
    factors[...] = jnp.zeros(factors.shape, BF16)
    packs[r] = jnp.zeros(packs.shape[1:], BF16)
    for m in range(steps):
        lanes = slice(m * rank, (m + 1) * rank)
        packs[r, :, half + m * rank : half + (m + 1) * rank] = dright_raw[0, m]
        for a in range(local_rows):
            dleft[a, :, lanes] = dleft_raw[a, m]
            factors[m, :, a * rank : (a + 1) * rank] = dright_raw[a, m]
    lead_left[at.z, at.x] = jnp.zeros(lead_left.shape[2:], BF16)
    for m in range(steps - 1):
        lead_left[at.z, at.x, :, m * rank : (m + 1) * rank] = dleft_raw[0, m]

    @pl.when(below)
    def _():
        lead_all.first()

    loads[3].wait()

    @pl.when(solving)
    def _():
        running["columns"] = at.start(column_copies, solving)
        columns[at.z] = inverse[r % steps, :, pl.ds(pl.multiple_of(at.z * LANES, LANES), LANES)]

    left_copies = at.start(left_copies)
    own_left[at.z] = dleft[at.z]
    for j in range(priors):
        own_up[j].wait_recv()
        over[1].append(go(share(at.down, j, 4, at.partner)))
        if j < priors // 2:
            relay.append(go(share(at.down, j, 2, at.up)))
        own_down[j].wait_recv()
        over[2].append(go(share(at.up, j, 5, at.partner)))
        if j >= priors // 2:
            relay.append(go(share(at.up, j, 2, at.down)))
        if j == LEAD_X_AT:

            @pl.when(below)
            def _():
                lead_all.second()

    loads[6].wait()
    whole_sides = sides_raw[...].astype(F32)
    for a in range(local_rows):
        sides[a] = whole_sides[:, a]

    for load in loads[4:6]:
        load.wait()
    for j in range(priors):
        relay[j].wait_recv()
        over[3].append(go(share(at.far, j, 6, at.partner)))
        for kind in range(4):
            over[kind][j].wait_recv()
        product = dot(right[:, j].reshape(-1, tile), known[j])
        coeff[:, pl.ds(j * rank, rank)] = product.astype(BF16).reshape(local_rows, rank, sides_count)

    def multiply(g):
        first = GROUPS[g][0]

        def one(i, carry):
            term = dot(left[i + first].reshape(priors * rank, tile), coeff[i + first], TN)
            term = term.astype(BF16).reshape(at.nz, NX, thin, sides_count)
            for at_x in range(NX):
                prior[g].parts[at_x, :, i] = term[:, at_x]
            return carry

        lax.fori_loop(0, len(GROUPS[g]), one, 0)

    def own_base(g):
        total = prior[g].result()
        for i, a in enumerate(GROUPS[g]):
            updated[a] = sides[a] - total[i]

    multiply(0)
    prior[0].first()
    @pl.when(below)
    def _():
        lead_all.wait()
        product = dot(inverse[r % steps], lead_left[...].reshape(tile, half))
        lane = lax.broadcasted_iota(jnp.int32, product.shape, 1)
        packs[r, :, :half] = jnp.where(lane < r * rank, product, 0.0).astype(BF16)
        for copy in pack_copies:
            copy.start()

    for k in range(1, steps):

        @pl.when(r != k)
        def _():
            remote(packs.at[k], packs.at[k], pack_send.at[1], pack_recv.at[k], at.next_r[1], c).wait_recv()

    cross.source[0] = jnp.zeros(cross.source.shape[1:], BF16)
    cross.out[...] = jnp.zeros(cross.out.shape, BF16)
    for k in range(1, steps):
        lanes = lanes_of(k)
        wide[:, lanes] = packs[k, :, : lanes.stop - lanes.start]
        cross.source[k] = packs[k, :, :half]
        for m in range(steps):
            first = (local_rows + k - 1) * rank
            factors[m, :, first : first + rank] = packs[k, :, half + m * rank : half + (m + 1) * rank]
    cross.feed()
    factor_copies = at.start(factor_copies)
    own_factors[at.x] = factors[at.x]
    multiply(1)
    multiply(2)
    prior[0].second()
    prior[1].first()
    own_base(0)
    @pl.when(solving)
    def _():
        base_block[at.x] = updated[0].astype(BF16)
        running["base"] = at.start(base_copies, solving)

    landed(factor_copies)
    cross.right(own_factors, local_rows, rank)
    multiply(3)
    @pl.when(solving)
    def _():
        landed(running["columns"])
        landed(running["base"])
        product = dot(columns[...].reshape(-1, LANES), base_block[...].reshape(-1, sides_count))
        start_parts[...] = product.astype(BF16).reshape(start_parts.shape)
        running["start"] = at.start(start_z_copies, solving)

    prior[1].second()
    prior[2].first()
    off = jnp.logical_and(at.z == 0, r <= at.x)
    @pl.when(solving)
    def _():
        landed(running["start"])
        total = start_parts[at.z].astype(F32)
        for d in range(1, at.nz):
            total = total + start_from[d].astype(F32)
        start[r % steps] = total.astype(BF16)
        for copy in start_copies:
            copy.start()

    prior[1].third()
    cross.share(off)
    cross.lead_z()
    for k in range(steps):

        @pl.when(r != k)
        def _():
            remote(start.at[k], start.at[k], start_send.at[1], start_recv.at[k], at.next_r[1], c).wait_recv()

    near.feed()
    prior[2].second()
    prior[3].first()
    near.right(own_factors, local_rows, rank)
    landed(left_copies)
    cross.left(own_left)
    prior[2].third()
    near.share(off)
    near.lead_z()
    prior[3].second()
    near.left(own_left)
    near.lead_x()
    cross.lead_x()
    prior[3].third()
    own_base(1)
    own_base(2)
    landed(cross.lead_copies)
    landed(cross.out_copies)
    landed(near.lead_copies)

    lead_coeff[...] = jnp.zeros(lead_coeff.shape, BF16)
    for m in range(steps - 1):
        for k in range(m + 1, steps):
            value = near.lead_rows(k, m)
            if m:
                lanes = lanes_of(m)
                size = lanes.stop - lanes.start
                value = value - dot(cross.lead_rows(k, m).astype(BF16)[:, :size], lead_coeff[lanes])
            first = lanes_of(k).start + m * rank
            lead_coeff[first : first + rank] = value.astype(BF16)
    for m in range(steps):
        answer = start[m].astype(F32)
        if m:
            answer = answer - dot(wide[:, lanes_of(m)], lead_coeff[lanes_of(m)])
        solved[m] = answer.astype(BF16)
    joined[...] = jnp.zeros(joined.shape, BF16)
    for m in range(1, steps):
        first = m * (m - 1) // 2 * rank
        joined[first : first + m * rank] = lead_coeff[lanes_of(m).start : lanes_of(m).start + m * rank]
    correction = dot(cross.whole[...].reshape(local_rows * thin, -1), joined[...])
    correction = correction.reshape(local_rows, thin, sides_count)
    own_base(3)
    landed(near.out_copies)
    for a in range(local_rows):
        updated[a] = updated[a] + (correction[a] - near.whole[a].astype(F32))

    for copy in at.sends:
        copy.close()

    @pl.when(below)
    def _():
        for copy in pack_copies:
            copy.wait_send()

    @pl.when(solving)
    def _():
        for copy in start_copies:
            copy.wait_send()


def place_results(updated, solved, updated_out, solved_out):
    for a in range(updated.shape[0]):
        updated_out[:, a] = updated[a]
    solved_out[...] = solved[...]


def local(right_sides, prior_left, prior_right, solved_prior, diag_left, diag_right, diag_inverse):
    thin, local_rows, sides = right_sides.shape
    priors, rank, tile = prior_left.shape[1:]
    diag_left, diag_right = jnp.swapaxes(diag_left, 2, 3), jnp.swapaxes(diag_right, 2, 3)
    steps = diag_left.shape[1]
    rows, cols = lax.axis_size(ROW), lax.axis_size(COL)
    nz = cols // NX
    width = steps * rank
    factor_width = (local_rows + NX - 1) * rank

    shapes = [
        prior_left.shape,
        prior_right.shape,
        (priors, tile, sides),
        (local_rows, priors * rank, sides),
        right_sides.shape,
        ((local_rows, thin, sides), F32),
        diag_left.shape,
        diag_right.shape,
        (local_rows, thin, width),
        diag_inverse.shape,
        (rows, thin, 4 * LANES),
        (nz, NX, thin, 2 * LANES),
        (steps, thin, factor_width),
        (NX, thin, factor_width),
        (nz, thin, width),
        (NX, thin, sides),
        (nz, thin, LANES),
        (nz, thin, sides),
        (nz, thin, sides),
        (thin, 4 * LANES),
        (4 * LANES, sides),
        (3 * LANES, sides),
    ]
    one = (len(GROUPS[0]), thin, sides)
    shapes += [(NX, nz, *one), (NX - 1, nz, *one), (nz, *one), (nz, *one)]
    for group in GROUPS[1:]:
        for lead in ((NX, nz), (nz // 2,), (nz // 2,), (nz,), (nz,), (nz,), (nz,)):
            shapes.append((*lead, len(group), thin, sides))
    for out, lead_lanes in ((3 * LANES, LANES), (sides, sides)):
        shapes += [
            (steps, thin, sides),
            (NX, thin, sides),
            (nz, rank, sides),
            (nz, rank, sides),
            (NX, rank, sides),
            (NX, nz, CHUNK, lead_lanes),
            (nz, thin, out),
            (nz, thin, out),
            (nz, CHUNK, lead_lanes),
            (nz, CHUNK, lead_lanes),
        ]
    scratch = [pltpu.VMEM(*shape) if isinstance(shape[0], tuple) else pltpu.VMEM(shape, BF16) for shape in shapes]
    bulk = len(GROUPS) - 1
    for shape in (
        (7,),
        (7, priors),
        (7, priors),
        (bulk, 6),
        (bulk, 6),
        (10, NX),
        (10, NX),
        (17, nz),
        (17, nz),
        (rows,),
        (steps,),
        (rows,),
        (steps,),
    ):
        scratch.append(pltpu.SemaphoreType.DMA(shape))
    updated, solved = pl.pallas_call(
        kernel,
        out_shape=(
            jax.ShapeDtypeStruct((local_rows, thin, sides), F32),
            jax.ShapeDtypeStruct((steps, thin, sides), BF16),
        ),
        in_specs=[pl.BlockSpec(memory_space=pl.ANY)] * 7,
        out_specs=(pl.BlockSpec(memory_space=pltpu.VMEM), pl.BlockSpec(memory_space=pltpu.VMEM)),
        scratch_shapes=scratch,
        compiler_params=pltpu.CompilerParams(
            collective_id=0, has_side_effects=True, vmem_limit_bytes=56 * 1024 * 1024
        ),
    )(right_sides, prior_left, prior_right, solved_prior, diag_left, diag_right, diag_inverse)
    return pl.pallas_call(
        place_results,
        out_shape=(
            jax.ShapeDtypeStruct((thin, local_rows, sides), F32),
            jax.ShapeDtypeStruct(solved.shape, BF16),
        ),
    )(updated, solved)


def solution(mesh):
    return jax.shard_map(
        local,
        mesh=mesh,
        in_specs=(
            P(COL, ROW, None),
            P(ROW, COL, None, None),
            P(ROW, COL, None, None),
            P(COL, ROW, None),
            P(ROW, None, None, COL),
            P(ROW, None, None, COL),
            P(None, COL, None),
        ),
        out_specs=(P(COL, ROW, None), P(None, COL, None)),
        check_vma=False,
    )
```

```python
import jax
import jax.numpy as jnp
from jax import lax
from jax.experimental import pallas as pl
from jax.experimental.pallas import tpu as pltpu
from jax.sharding import PartitionSpec as P

ROW = "row"
COL = "col"
CORES = 2
NX = 4
MESH = pl.DeviceIdType.MESH
F32 = jnp.float32
BF16 = jnp.bfloat16
LANES = 128
GROUPS = ((0,), (1, 2), (3, 4), (5, 6, 7))
CHUNK = 24
LEAD_X_AT = 3
TN = (((0,), (0,)), ((), ()))


def dot(a, b, dims=None):
    if dims is None:
        return jnp.dot(a, b, preferred_element_type=F32)
    return lax.dot_general(a, b, dims, preferred_element_type=F32)


def remote(src, dst, send, recv, row, col):
    return pltpu.make_async_remote_copy(
        src_ref=src,
        dst_ref=dst,
        send_sem=send,
        recv_sem=recv,
        device_id={ROW: row, COL: col},
        device_id_type=MESH,
    )


class Copy:
    def __init__(self, copy, only=None):
        self.copy, self.only, self.landed = copy, only, False

    def wait_recv(self):
        self.copy.wait_recv()
        self.landed = True

    def close(self):
        def rest():
            if not self.landed:
                self.copy.wait_recv()
            self.copy.wait_send()

        if self.only is None:
            rest()
        else:
            pl.when(self.only)(rest)


class Place:
    def __init__(self):
        self.rows, self.cols = lax.axis_size(ROW), lax.axis_size(COL)
        self.ny, self.nz = self.rows // CORES, self.cols // NX
        self.r, self.c = lax.axis_index(ROW), lax.axis_index(COL)
        self.y, self.q = self.r // CORES, self.r % CORES
        self.z, self.x = self.c // NX, self.c % NX
        self.up, self.down, self.far = (((self.y + d) % self.ny) * CORES + self.q for d in (1, self.ny - 1, 2))
        self.partner = self.y * CORES + 1 - self.q
        self.next_x = [(self.x + d) % NX for d in range(NX)]
        self.along_x = [self.z * NX + to for to in self.next_x]
        self.low, self.high = pl.ds(0, self.nz // 2), pl.ds(self.nz // 2, self.nz // 2)
        self.next_z = [(self.z + d) % self.nz for d in range(self.nz)]
        self.along_z = [to * NX + self.x for to in self.next_z]
        self.next_r = [(self.r + d) % self.rows for d in range(self.rows)]
        self.sends = []

    def go(self, copy, only=None):
        copy.start()
        tracked = Copy(copy, only)
        self.sends.append(tracked)
        return tracked

    def start(self, copies, only=None):
        return [self.go(copy, only) for copy in copies]

    def to_all_x(self, src, dst, sems):
        send, recv = sems
        return [
            remote(src(self.next_x[d]), dst(d), send.at[d], recv.at[d], self.r, self.along_x[d]) for d in (1, 3, 2)
        ]

    def to_all_z(self, src, dst, sems):
        send, recv = sems
        order = [4, 3, 5, 2, 6, 1, 7] if self.nz == 8 else range(1, self.nz)
        return [
            remote(src(self.next_z[d]), dst(d), send.at[d], recv.at[d], self.r, self.along_z[d]) for d in order
        ]


def landed(copies):
    for copy in copies:
        copy.wait_recv()


class Reduce:
    def __init__(self, at, buffers, x_sems, z_sems):
        self.at = at
        self.parts, self.from_a, self.from_b, self.from_l, self.from_r, self.part_sum, self.from_z = buffers
        self.x_send, self.x_recv = x_sems
        self.z_sems = z_sems
        self.copies = {}

    def send_x(self, kind, src, dst, d):
        at = self.at
        copy = remote(src, dst, self.x_send.at[kind], self.x_recv.at[kind], at.r, at.along_x[d])
        self.copies[kind] = at.go(copy)

    def first(self):
        at = self.at
        left, right, far = at.next_x[3], at.next_x[1], at.next_x[2]
        self.send_x(0, self.parts.at[far, at.low], self.from_a, 1)
        self.send_x(1, self.parts.at[far, at.high], self.from_b, 3)
        self.send_x(2, self.parts.at[right, at.high], self.from_l.at[at.high], 1)
        self.send_x(3, self.parts.at[left, at.low], self.from_r.at[at.low], 3)

    def second(self):
        at = self.at
        left, right = at.next_x[3], at.next_x[1]
        self.copies[0].wait_recv()
        own = self.parts[right, at.low].astype(F32)
        self.parts[right, at.low] = (own + self.from_a[...].astype(F32)).astype(BF16)
        self.send_x(4, self.parts.at[right, at.low], self.from_l.at[at.low], 1)
        self.copies[1].wait_recv()
        own = self.parts[left, at.high].astype(F32)
        self.parts[left, at.high] = (own + self.from_b[...].astype(F32)).astype(BF16)
        self.send_x(5, self.parts.at[left, at.high], self.from_r.at[at.high], 3)

    def third(self):
        at = self.at
        for kind in range(2, 6):
            self.copies[kind].wait_recv()

        def one(i, carry):
            total = self.parts[at.x, i].astype(F32) + self.from_l[i].astype(F32) + self.from_r[i].astype(F32)
            self.part_sum[i] = total.astype(BF16)
            return carry

        lax.fori_loop(0, at.nz, one, 0)
        self.send_z()

    def send_z(self):
        at = self.at
        self.z_copies = at.start(
            at.to_all_z(lambda to: self.part_sum.at[to], lambda d: self.from_z.at[d], self.z_sems)
        )

    def result(self):
        at = self.at
        landed(self.z_copies)
        total = self.part_sum[at.z].astype(F32)
        for d in range(1, at.nz):
            total = total + self.from_z[d].astype(F32)
        return total


class ReduceDirect(Reduce):
    def __init__(self, at, buffers, x_sems, z_sems):
        self.at = at
        self.parts, self.from_x, self.part_sum, self.from_z = buffers
        self.x_sems, self.z_sems = x_sems, z_sems

    def first(self):
        at = self.at
        self.x_copies = at.start(
            at.to_all_x(lambda to: self.parts.at[to], lambda d: self.from_x.at[d - 1], self.x_sems)
        )

    def second(self):
        at = self.at
        landed(self.x_copies)

        def one(i, carry):
            total = self.parts[at.x, i].astype(F32)
            for d in range(NX - 1):
                total = total + self.from_x[d, i].astype(F32)
            self.part_sum[i] = total.astype(BF16)
            return carry

        lax.fori_loop(0, at.nz, one, 0)
        self.send_z()


class Gather:
    def __init__(self, at, whole, x_sems, z_sems, only=None):
        self.at, self.whole, self.only = at, whole, only
        self.z_made = at.to_all_z(lambda to: whole.at[at.z, at.x], lambda d: whole.at[at.z, at.x], z_sems)
        self.x_made = at.to_all_x(lambda to: whole.at[:, at.x], lambda d: whole.at[:, at.x], x_sems)

    def first(self):
        self.z_copies = self.at.start(self.z_made, self.only)

    def second(self):
        landed(self.z_copies)
        self.x_copies = self.at.start(self.x_made, self.only)

    def wait(self):
        landed(self.x_copies)


class Flow:
    def __init__(self, at, buffers, sems, separate):
        self.at, self.separate = at, separate
        self.source, self.block, self.parts, self.from_z, self.steps, self.lead, self.out, self.whole = buffers[:8]
        self.lead_parts, self.lead_from_z = buffers[8:]
        self.sems = sems

    def feed(self):
        at = self.at
        self.block[at.x] = self.source[at.x]
        self.fed = at.start(
            at.to_all_x(lambda to: self.source.at[to], lambda d: self.block.at[at.x], self.sems[0])
        )

    def right(self, factors, positions, rank):
        at = self.at
        landed(self.fed)
        count, thin, sides = self.block.shape
        product = dot(factors[...].reshape(count * thin, -1), self.block[...].reshape(count * thin, sides), TN)
        self.parts[...] = product[: positions * rank].astype(BF16).reshape(positions, rank, sides)
        self.z_copies = at.start(
            at.to_all_z(lambda to: self.parts.at[to], lambda d: self.from_z.at[d], self.sems[1])
        )
        lead = product[positions * rank :]
        chunks = (NX - 1) * rank // CHUNK
        for i in range(at.nz):
            part = lead[i * CHUNK : (i + 1) * CHUNK] if i < chunks else jnp.zeros((CHUNK, sides), F32)
            self.lead_parts[i] = part[:, : self.lead_parts.shape[2]].astype(BF16)
        self.lead_sums = at.start(
            at.to_all_z(lambda to: self.lead_parts.at[to], lambda d: self.lead_from_z.at[d], self.sems[6])
        )

    def share(self, off):
        at = self.at
        landed(self.z_copies)
        total = self.parts[at.z].astype(F32)
        for d in range(1, at.nz):
            total = total + self.from_z[d].astype(F32)
        self.steps[at.x] = jnp.where(off, 0.0, total).astype(BF16)
        self.x_copies = at.start(
            at.to_all_x(lambda to: self.steps.at[at.x], lambda d: self.steps.at[at.x], self.sems[2])
        )

    def lead_z(self):
        at = self.at
        landed(self.lead_sums)
        total = self.lead_parts[at.z].astype(F32)
        for d in range(1, at.nz):
            total = total + self.lead_from_z[d].astype(F32)
        self.lead[at.x, at.z] = total.astype(BF16)
        own = self.lead.at[at.x, at.z]
        self.lead_all = at.start(at.to_all_z(lambda to: own, lambda d: own, self.sems[3]))

    def left(self, factors):
        at = self.at
        landed(self.x_copies)
        nz, thin, width = factors.shape
        rows = factors[...].reshape(nz * thin, width)
        rank = self.steps.shape[1]
        if self.separate:
            for m in range(1, NX):
                lanes = lanes_of(m)
                product = dot(rows[:, m * rank : (m + 1) * rank], self.steps[m, :, : lanes.stop - lanes.start])
                first = m * (m - 1) // 2 * rank
                product = product[:, : m * rank].astype(BF16).reshape(nz, thin, m * rank)
                self.out[:, :, first : first + m * rank] = product
        else:
            product = dot(rows, self.steps[...].reshape(width, -1))
            self.out[...] = product.astype(BF16).reshape(nz, thin, -1)
        self.whole[at.z] = self.out[at.z]
        self.out_copies = at.start(
            at.to_all_z(lambda to: self.out.at[to], lambda d: self.whole.at[at.z], self.sems[4])
        )

    def lead_x(self):
        at = self.at
        landed(self.lead_all)
        own = self.lead.at[at.x, pl.ds(0, (NX - 1) * self.steps.shape[1] // CHUNK)]
        self.lead_copies = at.start(at.to_all_x(lambda to: own, lambda d: own, self.sems[5]))

    def lead_rows(self, k, m):
        rank = self.steps.shape[1]
        pieces = rank // CHUNK
        first = (k - 1) * pieces
        return jnp.concatenate([self.lead[m, first + i].astype(F32) for i in range(pieces)], axis=0)


def lanes_of(m):
    first = (None, 0, LANES, 2 * LANES)[m]
    return slice(first, first + (LANES if m < 3 else 2 * LANES))


def take(refs, count):
    return [refs.pop(0) for _ in range(count)]


def kernel(sides_in, left_in, right_in, known_in, dleft_in, dright_in, inverse_in, updated, solved, *scratch):
    at = Place()
    r, c, go = at.r, at.c, at.go
    refs = list(scratch)
    left, right, known, coeff, sides_raw, sides, dleft_raw, dright_raw, dleft, inverse = take(refs, 10)
    packs, lead_left, factors, own_factors, own_left = take(refs, 5)
    base_block, columns, start_parts, start_from = take(refs, 4)
    wide, lead_coeff, joined = take(refs, 3)
    lead_buffers = take(refs, 4)
    bulk_buffers = [take(refs, 7) for _ in GROUPS[1:]]
    flow_buffers = [take(refs, 10) for _ in range(2)]
    start = flow_buffers[1][0]
    load_sem, gather_send, gather_recv, bulk_send, bulk_recv = take(refs, 5)
    x_send, x_recv, z_send, z_recv = take(refs, 4)
    pack_send, pack_recv, start_send, start_recv = take(refs, 4)
    x_sems = [(x_send.at[i], x_recv.at[i]) for i in range(x_send.shape[0])]
    z_sems = [(z_send.at[i], z_recv.at[i]) for i in range(z_send.shape[0])]

    depth, priors = known_in.shape[1], known_in.shape[0]
    local_rows, steps, thin, rank = dleft_in.shape
    sides_count = sides.shape[2]
    tile = left.shape[3]
    width = steps * rank
    half = packs.shape[2] // 2
    solving = r < steps
    below = jnp.logical_and(r > 0, solving)

    prior = [ReduceDirect(at, lead_buffers, x_sems.pop(), z_sems.pop())]
    for i, buffers in enumerate(bulk_buffers):
        prior.append(Reduce(at, buffers, (bulk_send.at[i], bulk_recv.at[i]), z_sems.pop()))
    lead_all = Gather(at, lead_left, x_sems.pop(), z_sems.pop(), below)
    base_copies = at.to_all_x(lambda to: base_block.at[at.x], lambda d: base_block.at[at.x], x_sems.pop())
    start_z_copies = at.to_all_z(lambda to: start_parts.at[to], lambda d: start_from.at[d], z_sems.pop())
    column_copies = at.to_all_z(
        lambda to: inverse.at[r % steps, :, pl.ds(pl.multiple_of(to * LANES, LANES), LANES)],
        lambda d: columns.at[at.z],
        z_sems.pop(),
    )
    start_copies = [
        remote(start.at[r % steps], start.at[r % steps], start_send.at[d], start_recv.at[r % steps], at.next_r[d], c)
        for d in range(1, at.rows)
    ]
    pack_copies = [
        remote(packs.at[r], packs.at[r], pack_send.at[d], pack_recv.at[r % steps], at.next_r[d], c)
        for d in range(1, at.rows)
    ]
    running = {}
    flows = [
        Flow(
            at,
            buffers,
            (x_sems.pop(), z_sems.pop(), x_sems.pop(), z_sems.pop(), z_sems.pop(), x_sems.pop(), z_sems.pop()),
            separate,
        )
        for buffers, separate in zip(flow_buffers, (True, False))
    ]
    cross, near = flows
    factor_copies = at.to_all_x(lambda to: factors.at[to], lambda d: own_factors.at[at.x], x_sems.pop())
    left_copies = at.to_all_z(lambda to: dleft.at[to], lambda d: own_left.at[at.z], z_sems.pop())

    loads = [
        pltpu.make_async_copy(src, dst, load_sem.at[i])
        for i, (src, dst) in enumerate(
            (
                (known_in, known.at[:, pl.ds(r * depth, depth)]),
                (dleft_in, dleft_raw),
                (dright_in, dright_raw),
                (inverse_in, inverse),
                (right_in, right),
                (left_in, left),
                (sides_in, sides_raw),
            )
        )
    ]
    for load in loads:
        load.start()
    barrier = pltpu.get_barrier_semaphore()
    peers = [(at.next_r[d], c) for d in range(1, at.rows)]
    peers += [(r, at.along_x[d]) for d in range(1, NX)]
    peers += [(r, at.along_z[d]) for d in range(1, at.nz)]
    for row, col in peers:
        pl.semaphore_signal(barrier, inc=1, device_id={ROW: row, COL: col}, device_id_type=MESH)

    loads[0].wait()
    pl.semaphore_wait(barrier, len(peers))

    def block(row, j):
        return known.at[j, pl.ds(row * depth, depth)]

    def share(row_of_block, j, kind, target):
        part = block(row_of_block, j)
        return remote(part, part, gather_send.at[kind, j], gather_recv.at[kind, j], target, c)

    own_up, own_down, relay, over = [], [], [], [[], [], [], []]
    for j in range(priors):
        own_up.append(go(share(r, j, 0, at.up)))
        own_down.append(go(share(r, j, 1, at.down)))
        over[0].append(go(share(r, j, 3, at.partner)))
    for load in loads[1:3]:
        load.wait()
    factors[...] = jnp.zeros(factors.shape, BF16)
    packs[r] = jnp.zeros(packs.shape[1:], BF16)
    for m in range(steps):
        lanes = slice(m * rank, (m + 1) * rank)
        packs[r, :, half + m * rank : half + (m + 1) * rank] = dright_raw[0, m]
        for a in range(local_rows):
            dleft[a, :, lanes] = dleft_raw[a, m]
            factors[m, :, a * rank : (a + 1) * rank] = dright_raw[a, m]
    lead_left[at.z, at.x] = jnp.zeros(lead_left.shape[2:], BF16)
    for m in range(steps - 1):
        lead_left[at.z, at.x, :, m * rank : (m + 1) * rank] = dleft_raw[0, m]

    @pl.when(below)
    def _():
        lead_all.first()

    loads[3].wait()

    @pl.when(solving)
    def _():
        running["columns"] = at.start(column_copies, solving)
        columns[at.z] = inverse[r % steps, :, pl.ds(pl.multiple_of(at.z * LANES, LANES), LANES)]

    left_copies = at.start(left_copies)
    own_left[at.z] = dleft[at.z]
    for j in range(priors):
        own_up[j].wait_recv()
        over[1].append(go(share(at.down, j, 4, at.partner)))
        if j < priors // 2:
            relay.append(go(share(at.down, j, 2, at.up)))
        own_down[j].wait_recv()
        over[2].append(go(share(at.up, j, 5, at.partner)))
        if j >= priors // 2:
            relay.append(go(share(at.up, j, 2, at.down)))
        if j == LEAD_X_AT:

            @pl.when(below)
            def _():
                lead_all.second()

    loads[6].wait()
    whole_sides = sides_raw[...].astype(F32)
    for a in range(local_rows):
        sides[a] = whole_sides[:, a]

    for load in loads[4:6]:
        load.wait()
    for j in range(priors):
        relay[j].wait_recv()
        over[3].append(go(share(at.far, j, 6, at.partner)))
        for kind in range(4):
            over[kind][j].wait_recv()
        product = dot(right[:, j].reshape(-1, tile), known[j])
        coeff[:, pl.ds(j * rank, rank)] = product.astype(BF16).reshape(local_rows, rank, sides_count)

    def multiply(g):
        first = GROUPS[g][0]

        def one(i, carry):
            term = dot(left[i + first].reshape(priors * rank, tile), coeff[i + first], TN)
            term = term.astype(BF16).reshape(at.nz, NX, thin, sides_count)
            for at_x in range(NX):
                prior[g].parts[at_x, :, i] = term[:, at_x]
            return carry

        lax.fori_loop(0, len(GROUPS[g]), one, 0)

    def own_base(g):
        total = prior[g].result()
        for i, a in enumerate(GROUPS[g]):
            updated[a] = sides[a] - total[i]

    multiply(0)
    prior[0].first()
    @pl.when(below)
    def _():
        lead_all.wait()
        product = dot(inverse[r % steps], lead_left[...].reshape(tile, half))
        lane = lax.broadcasted_iota(jnp.int32, product.shape, 1)
        packs[r, :, :half] = jnp.where(lane < r * rank, product, 0.0).astype(BF16)
        for copy in pack_copies:
            copy.start()

    for k in range(1, steps):

        @pl.when(r != k)
        def _():
            remote(packs.at[k], packs.at[k], pack_send.at[1], pack_recv.at[k], at.next_r[1], c).wait_recv()

    cross.source[0] = jnp.zeros(cross.source.shape[1:], BF16)
    cross.out[...] = jnp.zeros(cross.out.shape, BF16)
    for k in range(1, steps):
        lanes = lanes_of(k)
        wide[:, lanes] = packs[k, :, : lanes.stop - lanes.start]
        cross.source[k] = packs[k, :, :half]
        for m in range(steps):
            first = (local_rows + k - 1) * rank
            factors[m, :, first : first + rank] = packs[k, :, half + m * rank : half + (m + 1) * rank]
    cross.feed()
    factor_copies = at.start(factor_copies)
    own_factors[at.x] = factors[at.x]
    multiply(1)
    multiply(2)
    prior[0].second()
    prior[1].first()
    own_base(0)
    @pl.when(solving)
    def _():
        base_block[at.x] = updated[0].astype(BF16)
        running["base"] = at.start(base_copies, solving)

    landed(factor_copies)
    cross.right(own_factors, local_rows, rank)
    multiply(3)
    @pl.when(solving)
    def _():
        landed(running["columns"])
        landed(running["base"])
        product = dot(columns[...].reshape(-1, LANES), base_block[...].reshape(-1, sides_count))
        start_parts[...] = product.astype(BF16).reshape(start_parts.shape)
        running["start"] = at.start(start_z_copies, solving)

    prior[1].second()
    prior[2].first()
    off = jnp.logical_and(at.z == 0, r <= at.x)
    @pl.when(solving)
    def _():
        landed(running["start"])
        total = start_parts[at.z].astype(F32)
        for d in range(1, at.nz):
            total = total + start_from[d].astype(F32)
        start[r % steps] = total.astype(BF16)
        for copy in start_copies:
            copy.start()

    prior[1].third()
    cross.share(off)
    landed(left_copies)
    cross.left(own_left)
    cross.lead_z()
    for k in range(steps):

        @pl.when(r != k)
        def _():
            remote(start.at[k], start.at[k], start_send.at[1], start_recv.at[k], at.next_r[1], c).wait_recv()

    near.feed()
    prior[2].second()
    prior[3].first()
    near.right(own_factors, local_rows, rank)
    prior[2].third()
    near.share(off)
    near.lead_z()
    prior[3].second()
    near.left(own_left)
    near.lead_x()
    cross.lead_x()
    prior[3].third()
    own_base(1)
    own_base(2)
    landed(cross.lead_copies)
    landed(cross.out_copies)
    landed(near.lead_copies)

    lead_coeff[...] = jnp.zeros(lead_coeff.shape, BF16)
    for m in range(steps - 1):
        for k in range(m + 1, steps):
            value = near.lead_rows(k, m)
            if m:
                lanes = lanes_of(m)
                size = lanes.stop - lanes.start
                value = value - dot(cross.lead_rows(k, m).astype(BF16)[:, :size], lead_coeff[lanes])
            first = lanes_of(k).start + m * rank
            lead_coeff[first : first + rank] = value.astype(BF16)
    for m in range(steps):
        answer = start[m].astype(F32)
        if m:
            answer = answer - dot(wide[:, lanes_of(m)], lead_coeff[lanes_of(m)])
        solved[m] = answer.astype(BF16)
    joined[...] = jnp.zeros(joined.shape, BF16)
    for m in range(1, steps):
        first = m * (m - 1) // 2 * rank
        joined[first : first + m * rank] = lead_coeff[lanes_of(m).start : lanes_of(m).start + m * rank]
    correction = dot(cross.whole[...].reshape(local_rows * thin, -1), joined[...])
    correction = correction.reshape(local_rows, thin, sides_count)
    own_base(3)
    landed(near.out_copies)
    for a in range(local_rows):
        updated[a] = updated[a] + (correction[a] - near.whole[a].astype(F32))

    for copy in at.sends:
        copy.close()

    @pl.when(below)
    def _():
        for copy in pack_copies:
            copy.wait_send()

    @pl.when(solving)
    def _():
        for copy in start_copies:
            copy.wait_send()


def place_results(updated, solved, updated_out, solved_out):
    for a in range(updated.shape[0]):
        updated_out[:, a] = updated[a]
    solved_out[...] = solved[...]


def local(right_sides, prior_left, prior_right, solved_prior, diag_left, diag_right, diag_inverse):
    thin, local_rows, sides = right_sides.shape
    priors, rank, tile = prior_left.shape[1:]
    diag_left, diag_right = jnp.swapaxes(diag_left, 2, 3), jnp.swapaxes(diag_right, 2, 3)
    steps = diag_left.shape[1]
    rows, cols = lax.axis_size(ROW), lax.axis_size(COL)
    nz = cols // NX
    width = steps * rank
    factor_width = (local_rows + NX - 1) * rank

    shapes = [
        prior_left.shape,
        prior_right.shape,
        (priors, tile, sides),
        (local_rows, priors * rank, sides),
        right_sides.shape,
        ((local_rows, thin, sides), F32),
        diag_left.shape,
        diag_right.shape,
        (local_rows, thin, width),
        diag_inverse.shape,
        (rows, thin, 4 * LANES),
        (nz, NX, thin, 2 * LANES),
        (steps, thin, factor_width),
        (NX, thin, factor_width),
        (nz, thin, width),
        (NX, thin, sides),
        (nz, thin, LANES),
        (nz, thin, sides),
        (nz, thin, sides),
        (thin, 4 * LANES),
        (4 * LANES, sides),
        (3 * LANES, sides),
    ]
    one = (len(GROUPS[0]), thin, sides)
    shapes += [(NX, nz, *one), (NX - 1, nz, *one), (nz, *one), (nz, *one)]
    for group in GROUPS[1:]:
        for lead in ((NX, nz), (nz // 2,), (nz // 2,), (nz,), (nz,), (nz,), (nz,)):
            shapes.append((*lead, len(group), thin, sides))
    for out, lead_lanes in ((3 * LANES, LANES), (sides, sides)):
        shapes += [
            (steps, thin, sides),
            (NX, thin, sides),
            (nz, rank, sides),
            (nz, rank, sides),
            (NX, rank, sides),
            (NX, nz, CHUNK, lead_lanes),
            (nz, thin, out),
            (nz, thin, out),
            (nz, CHUNK, lead_lanes),
            (nz, CHUNK, lead_lanes),
        ]
    scratch = [pltpu.VMEM(*shape) if isinstance(shape[0], tuple) else pltpu.VMEM(shape, BF16) for shape in shapes]
    bulk = len(GROUPS) - 1
    for shape in (
        (7,),
        (7, priors),
        (7, priors),
        (bulk, 6),
        (bulk, 6),
        (10, NX),
        (10, NX),
        (17, nz),
        (17, nz),
        (rows,),
        (steps,),
        (rows,),
        (steps,),
    ):
        scratch.append(pltpu.SemaphoreType.DMA(shape))
    updated, solved = pl.pallas_call(
        kernel,
        out_shape=(
            jax.ShapeDtypeStruct((local_rows, thin, sides), F32),
            jax.ShapeDtypeStruct((steps, thin, sides), BF16),
        ),
        in_specs=[pl.BlockSpec(memory_space=pl.ANY)] * 7,
        out_specs=(pl.BlockSpec(memory_space=pltpu.VMEM), pl.BlockSpec(memory_space=pltpu.VMEM)),
        scratch_shapes=scratch,
        compiler_params=pltpu.CompilerParams(
            collective_id=0, has_side_effects=True, vmem_limit_bytes=56 * 1024 * 1024
        ),
    )(right_sides, prior_left, prior_right, solved_prior, diag_left, diag_right, diag_inverse)
    return pl.pallas_call(
        place_results,
        out_shape=(
            jax.ShapeDtypeStruct((thin, local_rows, sides), F32),
            jax.ShapeDtypeStruct(solved.shape, BF16),
        ),
    )(updated, solved)


def solution(mesh):
    return jax.shard_map(
        local,
        mesh=mesh,
        in_specs=(
            P(COL, ROW, None),
            P(ROW, COL, None, None),
            P(ROW, COL, None, None),
            P(COL, ROW, None),
            P(ROW, None, None, COL),
            P(ROW, None, None, COL),
            P(None, COL, None),
        ),
        out_specs=(P(COL, ROW, None), P(None, COL, None)),
        check_vma=False,
    )
```
